512 devices in a mesh: row: 16 (over y, z_hi, core), col: 32 (over x, z_lo).
Axes of the slice: x: 4, y: 4, z: 16 (z_hi: 2, z_lo: 8; z = z_hi * 8 + z_lo), core: 2. Of those that a mesh axis runs over, the one named last changes fastest.
Arguments:
- latent: bfloat16 [16, 64, 128, 320], P(None, 'row', 'col'), may hold values from -6 to 6
- conv_weight: bfloat16 [2, 3, 3, 320, 320], replicated, may hold values from -0.109375 to 0.109375
- conv_gain: float32 [2, 320], replicated, may hold values from 0.25 to 1.75
- qkv_weight: bfloat16 [3, 2048, 320], P(None, 'col'), may hold values from -0.3125 to 0.3125
- qk_gain: bfloat16 [2, 2048], P(None, 'col'), may hold values from 0.6 to 9, as said below
- out_weight: bfloat16 [2048, 320], P('col'), may hold values from -0.5 to 0.5
Outputs:
- features: bfloat16 [16, 64, 128, 320], P(None, 'row', 'col')
- mixed: bfloat16 [16, 32, 64, 320], P('row', None, 'col')
The draws below stay inside these ranges and needn't reach their ends.
Inputs may be any that keep to these rules, and one draw needn't show every extreme that they name: `qk_gain`: positive gains.
All inputs are finite; a program needn't handle non-finite values.
Results may differ from the reference program's by a relative error of at most 0.035.
Values may be sent and summed in bfloat16 or wider, within the bound.
No kernel may reach another device: no remote copies, remote signals or barrier semaphores. Data moves between devices by JAX's collectives and lax.ppermute only.
A program may use at most 64 MiB of HBM per device.

```python
import math
import jax
import jax.numpy as jnp
from jax import lax

C = 320
HD = 128
LAYERS = 2
IMAGES = 16
HEADS = 16
DM = 2048
H0 = 64
W0 = 128
H1 = 32
W1 = 64
KEYS = 2048


def draw_qk_gain(key, part):
    key_base = jax.random.fold_in(key, 0)
    base_gain = jnp.exp(jax.random.uniform(key_base, (2, DM), jnp.float32, math.log(0.6), math.log(1.8)))
    return base_gain.astype(jnp.bfloat16)


def block_levels(own_key, extent, cuts, low, largest):
    factor_of, own = 1.0, jax.random.fold_in(own_key, 6)
    for axis_at, parts in cuts:
        steps = jnp.exp(jax.random.uniform(jax.random.fold_in(own, axis_at), (parts,), jnp.float32, low / len(cuts), largest / len(cuts)))
        factor_of = factor_of * jnp.repeat(steps, extent[axis_at] // parts).reshape([-1 if axis == axis_at else 1 for axis in range(len(extent))])
    return factor_of


def gaussian(key, dims, deviation, bound, shards=(), held_as=jnp.bfloat16):
    factor_of = block_levels(key, dims, shards, -0.22, 0.18) if shards else 1.0
    entries = jax.random.normal(key, dims, jnp.float32) * deviation * factor_of
    return jnp.minimum(jnp.maximum(entries, -bound), bound).astype(held_as)


def setup_inputs(seed: int = 0) -> dict:
    keys = jax.random.split(jax.random.key(seed), 7)
    latent = gaussian(keys[0], (IMAGES, H0, W0, C), 1.0, 6.0, ((1, 16), (2, 32)))
    conv_weight = gaussian(keys[1], (LAYERS, 3, 3, C, C), (9 * C) ** -0.5, 0.109375)
    conv_gain = jnp.clip(1.0 + 0.15 * jax.random.normal(keys[2], (LAYERS, C), jnp.float32), 0.25, 1.75)
    qkv_weight = gaussian(keys[3], (3, DM, C), C ** -0.5, 0.3125, ((1, 32),))
    qk_gain = draw_qk_gain(jax.random.fold_in(keys[6], 71), 0)
    out_weight = gaussian(keys[5], (DM, C), HD ** -0.5, 0.5, ((0, 32),))
    return dict(latent=latent, conv_weight=conv_weight, conv_gain=conv_gain, qkv_weight=qkv_weight, qk_gain=qk_gain, out_weight=out_weight)


def rms_silu(hidden, gain_row):
    factor = lax.rsqrt(lax.optimization_barrier(jnp.mean(hidden * hidden, axis=-1, keepdims=True)) + 1e-06)
    return jax.nn.silu(hidden * factor * gain_row.astype(jnp.float32)).astype(jnp.bfloat16)

def conv_wrap(activation, kernels):
    height, width, channels = activation.shape
    total = jnp.zeros((height * width, kernels.shape[-1]), jnp.float32)
    for row_tap in range(3):
        for col_tap in range(3):
            moved = jnp.roll(activation, (1 - row_tap, 1 - col_tap), axis=(0, 1))
            total = total + jnp.dot(moved.reshape(height * width, channels), kernels[row_tap, col_tap], preferred_element_type=jnp.float32)
    return total.reshape(height, width, kernels.shape[-1])

def head_norm(projected, gain_row):
    factor = lax.rsqrt(lax.optimization_barrier(jnp.mean(projected * projected, axis=-1, keepdims=True)) + 1e-06)
    return (projected * factor * gain_row.astype(jnp.float32)).astype(jnp.bfloat16)

def project(source, matrix):
    return lax.dot_general(source, matrix, (((1,), (1,)), ((), ())), preferred_element_type=jnp.float32)

def reference(latent, conv_weight, conv_gain, qkv_weight, qk_gain, out_weight):
    head_weights = qkv_weight.reshape(3, HEADS, HD, C).transpose(1, 0, 2, 3)
    head_gains = qk_gain.reshape(2, HEADS, HD).transpose(1, 0, 2)
    head_out = out_weight.reshape(HEADS, HD, C)
    block_rows = math.gcd(KEYS, 512)
    scale = HD ** (-0.5)

    def one_image(image):
        hidden = image
        for layer_index in range(LAYERS):
            activation = rms_silu(hidden.astype(jnp.float32), conv_gain[layer_index])
            hidden = (hidden.astype(jnp.float32) + conv_wrap(activation, conv_weight[layer_index])).astype(jnp.bfloat16)
        pooled = hidden.astype(jnp.float32).reshape(H1, 2, W1, 2, C).mean(axis=(1, 3)).astype(jnp.bfloat16)
        token_rows = pooled.reshape(KEYS, C)

        def one_head(total, inputs):
            matrices, gains, out_rows = inputs
            query_norm = head_norm(project(token_rows, matrices[0]), gains[0])
            key_norm = head_norm(project(token_rows, matrices[1]), gains[1])
            value_rows = project(token_rows, matrices[2]).astype(jnp.bfloat16)

            def one_block(query_block):
                scores = jnp.dot(query_block, key_norm.T, preferred_element_type=jnp.float32) * scale
                shifted = jnp.exp(scores - lax.optimization_barrier(jnp.max(scores, axis=1, keepdims=True)))
                attended = jnp.dot(shifted.astype(jnp.bfloat16), value_rows, preferred_element_type=jnp.float32) / lax.optimization_barrier(jnp.sum(shifted, axis=1, keepdims=True))
                return jnp.dot(attended.astype(jnp.bfloat16), out_rows, preferred_element_type=jnp.float32)
            outputs = lax.map(one_block, query_norm.reshape(KEYS // block_rows, block_rows, HD))
            return (total + outputs.reshape(KEYS, C), None)
        summed, _ = lax.scan(one_head, jnp.zeros((KEYS, C), jnp.float32), (head_weights, head_gains, head_out))
        mixed = (token_rows.astype(jnp.float32) + summed).astype(jnp.bfloat16).reshape(H1, W1, C)
        return (hidden, mixed)
    features, mixed = lax.map(one_image, latent)
    return (features, mixed)
```

```python
import jax
import jax.numpy as jnp
from jax import lax
from jax.sharding import Mesh
from jax.sharding import PartitionSpec as P

SIZES = {"y": 4, "h": 2, "c": 2, "x": 4, "l": 8}
ROW = ("y", "h", "c")
COL = ("x", "l")
DEPTH = ("h", "l")
PLANE = ("x", "y", "c")


def move(array, axes, target):
    sizes = [SIZES[axis] for axis in axes]
    pairs = []
    count = 1
    for size in sizes:
        count *= size
    for index in range(count):
        rest, place = index, []
        for size in reversed(sizes):
            place.insert(0, rest % size)
            rest //= size
        flat = 0
        for size, value in zip(sizes, target(*place)):
            flat = flat * size + value % size
        pairs.append((index, flat))
    return lax.ppermute(array, axes, pairs)


def exchange(array, axes):
    return lax.all_to_all(array, axes, split_axis=0, concat_axis=0, tiled=True)


def rms_silu(hidden, gain_row):
    factor = lax.rsqrt(jnp.mean(hidden * hidden, axis=-1, keepdims=True) + 1e-06)
    return jax.nn.silu(hidden * factor * gain_row).astype(jnp.bfloat16)


def conv_layer(hidden, gain_row, kernels):
    strips, rows, cols, channels = hidden.shape
    wide = hidden.astype(jnp.float32)
    act = rms_silu(wide, gain_row)
    total = jnp.zeros((strips * (rows - 2) * (cols - 2), channels), jnp.float32)
    for a in range(3):
        for b in range(3):
            window = act[:, a : a + rows - 2, b : b + cols - 2].reshape(-1, channels)
            total = total + jnp.dot(window, kernels[a, b], preferred_element_type=jnp.float32)
    total = total.reshape(strips, rows - 2, cols - 2, channels)
    return (wide[:, 1:-1, 1:-1] + total).astype(jnp.bfloat16)


def head_norm(projected, gain_row):
    factor = lax.rsqrt(jnp.mean(projected * projected, axis=-1, keepdims=True) + 1e-06)
    return (projected * factor * gain_row.astype(jnp.float32)).astype(jnp.bfloat16)


def project(source, matrix):
    return lax.dot_general(
        source, matrix, (((1,), (1,)), ((), ())), preferred_element_type=jnp.float32
    )


def source_plane(y, h, l, step):
    depth = 8 * h + l + 2 * y - 4 + step
    return l // 2, (depth // 8) % 2, depth % 8


def shards(latent, conv_weight, conv_gain, qkv_weight, qk_gain, out_weight):
    channels = latent.shape[-1]
    core = lax.axis_index("c")
    first = core == 0

    slots = latent.reshape(4, 2, 2, 4, 4, channels).transpose(1, 0, 2, 3, 4, 5)
    tiles = exchange(slots.reshape(16, 4, 4, channels), DEPTH)

    gains = jnp.pad(qk_gain.reshape(1, 128), ((0, 15), (0, channels - 128)))
    packed = jnp.concatenate([qkv_weight.reshape(192, channels), out_weight, gains], 0)
    packed, tiles = lax.optimization_barrier((packed, tiles))
    parts = [
        move(packed, ("y", "h", "l"), lambda y, h, l, s=step: source_plane(y, h, l, s))
        for step in range(2)
    ]

    own = tiles.reshape(2, 8, 4, 4, channels).transpose(0, 2, 1, 3, 4).reshape(8, 32, channels)
    far = lax.ppermute(jnp.where(first, own[2:8], own[0:6]), "c", [(0, 1), (1, 0)])
    edge = move(
        jnp.where(first, own[0:2], own[6:8]), ("y", "c"), lambda y, c: (y - 1 + 2 * c, 1 - c)
    )
    top_0 = jnp.where(first, edge, far[0:2])
    low_0 = jnp.where(first, far[0:2], far[2:4])
    top_1 = jnp.where(first, far[2:4], far[4:6])
    low_1 = jnp.where(first, far[4:6], edge)
    block = jnp.concatenate([top_0, own[0:4], low_0, top_1, own[4:8], low_1], 0)
    block = block.reshape(2, 8, 32, channels)
    before = move(block[:, :, 30:32], ("x",), lambda x: (x + 1,))
    after = move(block[:, :, 0:2], ("x",), lambda x: (x - 1,))
    block = jnp.concatenate([before, block, after], 2)

    hidden = conv_layer(block, conv_gain[0], conv_weight[0])
    hidden = conv_layer(hidden, conv_gain[1], conv_weight[1])
    pooled = (
        hidden.astype(jnp.float32)
        .reshape(2, 2, 2, 16, 2, channels)
        .mean(axis=(2, 4))
        .astype(jnp.bfloat16)
        .reshape(64, channels)
    )

    tokens = exchange(jnp.broadcast_to(pooled[None], (16, 64, channels)), ("x", "y"))
    tokens = tokens.reshape(1024, channels)

    back = hidden.reshape(2, 4, 8, 4, channels).transpose(0, 2, 1, 3, 4)
    back = exchange(back.reshape(16, 4, 4, channels), DEPTH)
    features = back.reshape(2, 4, 2, 4, 4, channels).transpose(1, 0, 2, 3, 4, 5)
    features = features.reshape(16, 4, 4, channels)

    even = lax.axis_index("l") % 2 == 0
    lower = jnp.where(even, parts[0], parts[1])
    upper = jnp.where(even, parts[1], parts[0])

    def joined(start, length=64):
        return jnp.concatenate([lower[start : start + length], upper[start : start + length]], 0)

    query_gain = jnp.concatenate([lower[256, 0:64], upper[256, 0:64]])
    key_gain = jnp.concatenate([lower[256, 64:128], upper[256, 64:128]])
    query_norm = head_norm(project(tokens, joined(0)), query_gain)
    key_norm = head_norm(project(tokens, joined(64)), key_gain)
    value_rows = project(tokens, joined(128)).astype(jnp.bfloat16)
    pair = jnp.concatenate([key_norm, value_rows], 1)
    pair = jnp.concatenate([pair, lax.ppermute(pair, "c", [(0, 1), (1, 0)])], 0)
    keys, values = pair[:, :128], pair[:, 128:]

    scores = project(query_norm, keys) * (128 ** (-0.5))
    shifted = jnp.exp(scores - jnp.max(scores, axis=1, keepdims=True))
    attended = jnp.dot(shifted.astype(jnp.bfloat16), values, preferred_element_type=jnp.float32)
    attended = (attended / jnp.sum(shifted, axis=1, keepdims=True)).astype(jnp.bfloat16)
    terms = jnp.dot(attended, joined(192), preferred_element_type=jnp.float32)
    terms = (terms + tokens.astype(jnp.float32) * 0.0625).astype(jnp.bfloat16)

    terms = terms.reshape(4, 16, 8, 2, channels).transpose(0, 2, 1, 3, 4)
    terms = exchange(terms.reshape(32, 32, channels), PLANE)
    summed = terms.reshape(16, 2, 4, 2, 2, 2, channels).astype(jnp.float32).sum(0)
    mixed = summed.transpose(1, 2, 0, 3, 4, 5).reshape(64, channels).astype(jnp.bfloat16)
    mixed = move(
        mixed,
        ("y", "h", "c", "x", "l"),
        lambda y, h, c, x, l: (l // 2, h, l % 2, x, 2 * y + c),
    )
    return (features, mixed.reshape(1, 32, 2, channels))


def solution(mesh):
    planes = Mesh(mesh.devices.reshape(tuple(SIZES.values())), tuple(SIZES))
    placed = (
        P(None, ROW, COL, None),
        P(),
        P(),
        P(None, COL, None),
        P(None, COL),
        P(COL, None),
    )
    return jax.shard_map(
        shards,
        mesh=planes,
        in_specs=placed,
        out_specs=(P(None, ROW, COL, None), P(ROW, None, COL, None)),
        check_vma=False,
    )
```

```python
import jax
import jax.numpy as jnp
from jax import lax
from jax.experimental import pallas as pl
from jax.experimental.pallas import tpu as pltpu
from jax.sharding import Mesh
from jax.sharding import PartitionSpec as P


SIZES = {"y": 4, "h": 2, "c": 2, "x": 4, "l": 8}
ROW = ("y", "h", "c")
COL = ("x", "l")
DEPTH = ("h", "l")
PLANE = ("x", "y", "c")
C = 320
BF = jnp.bfloat16
F32 = jnp.float32


def move(array, axes, target):
    sizes = [SIZES[axis] for axis in axes]
    pairs = []
    count = 1
    for size in sizes:
        count *= size
    for index in range(count):
        rest, place = index, []
        for size in reversed(sizes):
            place.insert(0, rest % size)
            rest //= size
        flat = 0
        for size, value in zip(sizes, target(*place)):
            flat = flat * size + value % size
        pairs.append((index, flat))
    return lax.ppermute(array, axes, pairs)


def exchange(array, axes):
    return lax.all_to_all(array, axes, split_axis=0, concat_axis=0, tiled=True)


def swap(array):
    return lax.ppermute(array, "c", [(0, 1), (1, 0)])


def dot(left, right):
    return jnp.dot(left, right, preferred_element_type=F32)


def dot_t(left, right):
    return lax.dot_general(left, right, (((1,), (1,)), ((), ())), preferred_element_type=F32)


def conv_kernel(block, before, after, kernels, gains, feat_out, pool_out, held, act, taps):
    held[0:32] = before[...].reshape(32, C).astype(F32)
    held[32:544] = block[...].reshape(512, C).astype(F32)
    held[544:576] = after[...].reshape(32, C).astype(F32)
    held[576:608] = jnp.zeros((32, C), F32)
    act[576:608] = jnp.zeros((32, C), F32)
    for layer in range(2):
        rows = 576 - 32 * layer
        wide = held[0:rows]
        factor = lax.rsqrt(jnp.mean(wide * wide, axis=-1, keepdims=True) + 1e-06)
        scaled = wide * factor * gains[layer : layer + 1]
        act[0:rows] = scaled * jax.nn.sigmoid(scaled)
        for a in range(3):
            taps[0:rows, a * C : (a + 1) * C] = act[a : a + rows].astype(BF)
        out = rows - 32
        total = dot(taps[0:out], kernels[layer, 0])
        total = total + dot(taps[16 : 16 + out], kernels[layer, 1])
        total = total + dot(taps[32 : 32 + out], kernels[layer, 2])
        fresh = (held[17 : 17 + out] + total).astype(BF)
        if layer == 0:
            held[0:out] = fresh.astype(F32)
    place = lax.broadcasted_iota(jnp.int32, (256, 512), 1)
    index = lax.broadcasted_iota(jnp.int32, (256, 512), 0)
    source = (((index >> 4) & 7) * 4 + (index & 3)) * 16 + (index >> 7) * 8 + ((index >> 2) & 3)
    feat_out[...] = dot((place == source).astype(F32).astype(BF), fresh).astype(BF)
    place, index = place[0:64], index[0:64]
    same = ((place >> 5) == (index >> 3) * 2 + (index & 1)) & (
        ((place >> 1) & 7) == ((index >> 2) & 1) * 4 + ((index >> 1) & 1)
    )
    pooled = dot(jnp.where(same, 0.25, 0.0).astype(BF), fresh).astype(BF)
    for copy in range(16):
        pool_out[copy] = pooled


def conv_stack(block, before, after, kernels, gains):
    return pl.pallas_call(
        conv_kernel,
        out_shape=(
            jax.ShapeDtypeStruct((256, C), BF),
            jax.ShapeDtypeStruct((16, 64, C), BF),
        ),
        scratch_shapes=[
            pltpu.VMEM((608, C), F32),
            pltpu.VMEM((608, C), F32),
            pltpu.VMEM((576, 3 * C), BF),
        ],
        cost_estimate=pl.CostEstimate(
            flops=2 * 1056 * 9 * C * C, bytes_accessed=5_000_000, transcendentals=360_000
        ),
        compiler_params=pltpu.CompilerParams(vmem_limit_bytes=24 << 20),
        name="conv_stack",
    )(block, before, after, kernels, gains)


def norm(projected, gain):
    factor = lax.rsqrt(jnp.mean(projected * projected, axis=-1, keepdims=True) + 1e-06)
    return (projected * factor * gain).astype(BF)


def heads_kernel(tokens, near, far, query_out, pair_out):
    def both(start):
        return jnp.concatenate([near[start : start + 64], far[start : start + 64]], 0)

    matrix = jnp.concatenate([both(0), both(64), both(128)], 0)
    projected = dot_t(tokens[...], matrix)
    query_gain = near[256:257, 0:128].astype(F32) + far[257:258, 0:128].astype(F32)
    key_gain = near[258:259, 0:128].astype(F32) + far[259:260, 0:128].astype(F32)
    query_out[...] = norm(projected[:, 0:128], query_gain)
    pair_out[:, 0:128] = norm(projected[:, 128:256], key_gain)
    pair_out[:, 128:256] = projected[:, 256:384].astype(BF)


def heads(tokens, near, far):
    return pl.pallas_call(
        heads_kernel,
        out_shape=(
            jax.ShapeDtypeStruct((1024, 128), BF),
            jax.ShapeDtypeStruct((1024, 256), BF),
        ),
        cost_estimate=pl.CostEstimate(
            flops=2 * 1024 * 384 * C, bytes_accessed=2_000_000, transcendentals=2048
        ),
        compiler_params=pltpu.CompilerParams(vmem_limit_bytes=16 << 20),
        name="heads",
    )(tokens, near, far)


def attend_kernel(query, pair, pair_far, tokens, near, far, terms_out):
    head_out = jnp.concatenate([near[192:256], far[192:256]], 0)
    scale = 128 ** (-0.5)

    def one_block(step, _):
        rows = pl.ds(pl.multiple_of(step * 256, 256), 256)
        asked = query[rows]
        scores_near = dot_t(asked, pair[:, 0:128])
        scores_far = dot_t(asked, pair_far[:, 0:128])
        top = jnp.maximum(
            jnp.max(scores_near, axis=1, keepdims=True), jnp.max(scores_far, axis=1, keepdims=True)
        )
        shifted_near = jnp.exp((scores_near - top) * scale)
        shifted_far = jnp.exp((scores_far - top) * scale)
        total = jnp.sum(shifted_near, axis=1, keepdims=True) + jnp.sum(
            shifted_far, axis=1, keepdims=True
        )
        attended = dot(shifted_near.astype(BF), pair[:, 128:256])
        attended = attended + dot(shifted_far.astype(BF), pair_far[:, 128:256])
        attended = (attended / total).astype(BF)
        terms = dot(attended, head_out) + tokens[rows].astype(F32) * 0.0625
        for column in range(8):
            parts = [
                terms[y * 64 + column * 8 : y * 64 + column * 8 + 8] for y in range(4)
            ]
            terms_out[step * 8 + column] = jnp.concatenate(parts, 0).astype(BF)
        return 0

    lax.fori_loop(0, 4, one_block, 0)


def attend(query, pair, pair_far, tokens, near, far):
    return pl.pallas_call(
        attend_kernel,
        out_shape=jax.ShapeDtypeStruct((32, 32, C), BF),
        cost_estimate=pl.CostEstimate(
            flops=2 * 1024 * 128 * (2 * 2048 + C),
            bytes_accessed=3_000_000,
            transcendentals=1024 * 2048,
        ),
        compiler_params=pltpu.CompilerParams(vmem_limit_bytes=24 << 20),
        name="attend",
    )(query, pair, pair_far, tokens, near, far)


def sum_kernel(terms, mixed_out):
    total = terms[0].astype(F32)
    for head in range(1, 16):
        total = total + terms[head].astype(F32)
    mixed_out[...] = total.astype(BF)


def sum_heads(terms):
    return pl.pallas_call(
        sum_kernel,
        out_shape=jax.ShapeDtypeStruct((64, C), BF),
        cost_estimate=pl.CostEstimate(
            flops=16 * 64 * C, bytes_accessed=700_000, transcendentals=0
        ),
        compiler_params=pltpu.CompilerParams(vmem_limit_bytes=8 << 20),
        name="sum_heads",
    )(terms)


def nearest_plane(y, h, c, l):
    depth = 8 * h + l + 2 * y - 4 + c
    return l // 2, depth // 8, c, depth % 8


def plan(latent, conv_weight, conv_gain, qkv_weight, qk_gain, out_weight):
    first = lax.axis_index("c") == 0
    kernels = conv_weight.transpose(0, 2, 1, 3, 4).reshape(2, 3, 3 * C, C)

    tiles = exchange(latent, DEPTH)

    gains = qk_gain.reshape(2, 1, 64)
    gains = jnp.concatenate([jnp.pad(gains, ((0, 0), (0, 0), (0, 64))), jnp.pad(gains, ((0, 0), (0, 0), (64, 0)))], 1)
    gains = jnp.pad(gains.reshape(4, 128), ((0, 12), (0, C - 128)))
    packed = jnp.concatenate([qkv_weight.reshape(192, C), out_weight, gains], 0)
    near = move(packed, ("y", "h", "c", "l"), nearest_plane)
    far = swap(near)
    near, far = jnp.where(first, near, far), jnp.where(first, far, near)

    own = tiles.reshape(2, 8, 4, 4, C).transpose(1, 3, 0, 2, 4).reshape(32, 8, C)
    sides = swap(jnp.where(first, own[:, 2:8], own[:, 0:6]))
    edge = move(
        jnp.where(first, own[:, 0:2], own[:, 6:8]), ("y", "c"), lambda y, c: (y - 1 + 2 * c, 1 - c)
    )
    block = jnp.where(
        first,
        jnp.concatenate([edge, own[:, 0:4], sides[:, 0:4], own[:, 4:8], sides[:, 4:6]], 1),
        jnp.concatenate([sides[:, 0:2], own[:, 0:4], sides[:, 2:6], own[:, 4:8], edge], 1),
    )
    before = move(block[30:32], ("x",), lambda x: (x + 1,))
    after = move(block[0:2], ("x",), lambda x: (x - 1,))

    feature_tiles, pooled = conv_stack(block, before, after, kernels, conv_gain)

    tokens = exchange(pooled, ("x", "y")).reshape(1024, C)
    features = exchange(feature_tiles.reshape(16, 4, 4, C), DEPTH)

    query, pair = heads(tokens, near, far)
    pair_far = swap(pair)
    terms = attend(query, pair, pair_far, tokens, near, far)
    terms = exchange(terms, PLANE)
    mixed = sum_heads(terms.reshape(16, 64, C))
    mixed = move(
        mixed,
        ("y", "h", "c", "x", "l"),
        lambda y, h, c, x, l: (2 * h + l // 4, (l // 2) % 2, l % 2, x, 2 * y + c),
    )
    mixed = mixed.reshape(2, 8, 2, 2, C).transpose(1, 0, 2, 3, 4)
    return (features, mixed.reshape(1, 32, 2, C))


def solution(mesh):
    planes = Mesh(mesh.devices.reshape(tuple(SIZES.values())), tuple(SIZES))
    placed = (
        P(None, ROW, COL, None),
        P(),
        P(),
        P(None, COL, None),
        P(None, COL),
        P(COL, None),
    )
    return jax.shard_map(
        plan,
        mesh=planes,
        in_specs=placed,
        out_specs=(P(None, ROW, COL, None), P(ROW, None, COL, None)),
        check_vma=False,
    )
```

```python
import jax
import jax.numpy as jnp
from jax import lax
from jax.experimental import pallas as pl
from jax.experimental.pallas import tpu as pltpu
from jax.sharding import Mesh
from jax.sharding import PartitionSpec as P


SIZES = {"y": 4, "h": 2, "c": 2, "x": 4, "l": 8}
ROW = ("y", "h", "c")
COL = ("x", "l")
DEPTH = ("h", "l")
PLANE = ("x", "y", "c")
C = 320
BF = jnp.bfloat16
F32 = jnp.float32


def move(array, axes, target):
    sizes = [SIZES[axis] for axis in axes]
    pairs = []
    count = 1
    for size in sizes:
        count *= size
    for index in range(count):
        rest, place = index, []
        for size in reversed(sizes):
            place.insert(0, rest % size)
            rest //= size
        flat = 0
        for size, value in zip(sizes, target(*place)):
            flat = flat * size + value % size
        pairs.append((index, flat))
    return lax.ppermute(array, axes, pairs)


def exchange(array, axes):
    return lax.all_to_all(array, axes, split_axis=0, concat_axis=0, tiled=True)


def swap(array):
    return lax.ppermute(array, "c", [(0, 1), (1, 0)])


def dot(left, right):
    return jnp.dot(left, right, preferred_element_type=F32)


def dot_t(left, right):
    return lax.dot_general(left, right, (((1,), (1,)), ((), ())), preferred_element_type=F32)


def picked(core, first, count, own, other, edge):
    place = lax.broadcasted_iota(jnp.int32, (count * 16, 1), 0)
    column = first + (place >> 4)
    row = ((place >> 3) & 1) * 8 + (place & 7) + core * 4 - 2
    local = column * 8 + ((row >> 3) & 1) * 4 + (row & 3)
    near = jnp.where(((row >> 2) & 1) == core, local, local + 256)
    source = jnp.where((row < 0) | (row > 15), 512 + column * 2 + (row & 1), near)
    at = lax.broadcasted_iota(jnp.int32, (count * 16, 576), 1)
    choice = (at == source).astype(F32).astype(BF)
    rows = dot(choice[:, 0:256], own[...].reshape(256, C))
    rows = rows + dot(choice[:, 256:512], other[...].reshape(256, C))
    return rows + dot(choice[:, 512:576], edge[...])


def border_kernel(core, own, other, edge, left_out, right_out):
    left_out[...] = picked(core[0], 0, 2, own, other, edge).astype(BF)
    right_out[...] = picked(core[0], 30, 2, own, other, edge).astype(BF)


def border(core, own, other, edge):
    return pl.pallas_call(
        border_kernel,
        out_shape=(jax.ShapeDtypeStruct((32, C), BF),) * 2,
        in_specs=[pl.BlockSpec(memory_space=pltpu.SMEM)] + [pl.BlockSpec(memory_space=pltpu.VMEM)] * 3,
        compiler_params=pltpu.CompilerParams(vmem_limit_bytes=8 << 20),
        cost_estimate=pl.CostEstimate(
            flops=2 * 64 * 576 * C, bytes_accessed=400_000, transcendentals=0
        ),
        name="border",
    )(core, own, other, edge)


def conv_kernel(
    core, own, other, edge, before, after, gains, stored, feat_out, pool_out, held, act, taps, kernels, arrived
):
    fetches = [
        pltpu.make_async_copy(stored.at[layer], kernels.at[layer], arrived.at[layer]) for layer in range(2)
    ]
    for fetch in fetches:
        fetch.start()
    held[0:32] = before[...].astype(F32)
    held[32:544] = picked(core[0], 0, 32, own, other, edge)
    held[544:576] = after[...].astype(F32)
    held[576:608] = jnp.zeros((32, C), F32)
    act[576:608] = jnp.zeros((32, C), F32)
    for layer in range(2):
        rows = 576 - 32 * layer
        wide = held[0:rows]
        factor = lax.rsqrt(jnp.mean(wide * wide, axis=-1, keepdims=True) + 1e-06)
        scaled = wide * factor * gains[layer : layer + 1]
        act[0:rows] = scaled * jax.nn.sigmoid(scaled)
        for a in range(3):
            taps[0:rows, a * C : (a + 1) * C] = act[a : a + rows].astype(BF)
        out = rows - 32
        fetches[layer].wait()
        total = dot(taps[0:out], kernels[layer, :, 0].reshape(3 * C, C))
        total = total + dot(taps[16 : 16 + out], kernels[layer, :, 1].reshape(3 * C, C))
        total = total + dot(taps[32 : 32 + out], kernels[layer, :, 2].reshape(3 * C, C))
        fresh = (held[17 : 17 + out] + total).astype(BF)
        if layer == 0:
            held[0:out] = fresh.astype(F32)
    place = lax.broadcasted_iota(jnp.int32, (256, 512), 1)
    index = lax.broadcasted_iota(jnp.int32, (256, 512), 0)
    source = (((index >> 4) & 7) * 4 + (index & 3)) * 16 + (index >> 7) * 8 + ((index >> 2) & 3)
    feat_out[...] = dot((place == source).astype(F32).astype(BF), fresh).astype(BF)
    place, index = place[0:64], index[0:64]
    same = ((place >> 5) == (index >> 3) * 2 + (index & 1)) & (
        ((place >> 1) & 7) == ((index >> 2) & 1) * 4 + ((index >> 1) & 1)
    )
    pooled = dot(jnp.where(same, 0.25, 0.0).astype(BF), fresh).astype(BF)
    for copy in range(16):
        pool_out[copy] = pooled


def conv_stack(core, own, other, edge, before, after, kernels, gains):
    return pl.pallas_call(
        conv_kernel,
        out_shape=(
            jax.ShapeDtypeStruct((256, C), BF),
            jax.ShapeDtypeStruct((16, 64, C), BF),
        ),
        in_specs=[pl.BlockSpec(memory_space=pltpu.SMEM)]
        + [pl.BlockSpec(memory_space=pltpu.VMEM)] * 6
        + [pl.BlockSpec(memory_space=pltpu.HBM)],
        scratch_shapes=[
            pltpu.VMEM((608, C), F32),
            pltpu.VMEM((608, C), F32),
            pltpu.VMEM((576, 3 * C), BF),
            pltpu.VMEM((2, 3, 3, C, C), BF),
            pltpu.SemaphoreType.DMA((2,)),
        ],
        cost_estimate=pl.CostEstimate(
            flops=2 * 1056 * 9 * C * C, bytes_accessed=5_000_000, transcendentals=360_000
        ),
        compiler_params=pltpu.CompilerParams(vmem_limit_bytes=52 << 20),
        name="conv_stack",
    )(core, own, other, edge, before, after, gains, kernels)


def norm(projected, gain):
    factor = lax.rsqrt(jnp.mean(projected * projected, axis=-1, keepdims=True) + 1e-06)
    return (projected * factor * gain).astype(BF)


def heads_kernel(tokens, near, far, query_out, pair_out):
    def both(start):
        return jnp.concatenate([near[start : start + 64], far[start : start + 64]], 0)

    matrix = jnp.concatenate([both(0), both(64), both(128)], 0)
    projected = dot_t(tokens[...], matrix)
    query_gain = near[256:257, 0:128].astype(F32) + far[257:258, 0:128].astype(F32)
    key_gain = near[258:259, 0:128].astype(F32) + far[259:260, 0:128].astype(F32)
    query_out[...] = norm(projected[:, 0:128], query_gain)
    pair_out[:, 0:128] = norm(projected[:, 128:256], key_gain)
    pair_out[:, 128:256] = projected[:, 256:384].astype(BF)


def heads(tokens, near, far):
    return pl.pallas_call(
        heads_kernel,
        out_shape=(
            jax.ShapeDtypeStruct((1024, 128), BF),
            jax.ShapeDtypeStruct((1024, 256), BF),
        ),
        cost_estimate=pl.CostEstimate(
            flops=2 * 1024 * 384 * C, bytes_accessed=2_000_000, transcendentals=2048
        ),
        compiler_params=pltpu.CompilerParams(vmem_limit_bytes=16 << 20),
        name="heads",
    )(tokens, near, far)


def attend_kernel(query, pair, pair_far, tokens, near, far, terms_out):
    head_out = jnp.concatenate([near[192:256], far[192:256]], 0)
    scale = 128 ** (-0.5)

    def one_block(step, _):
        rows = pl.ds(pl.multiple_of(step * 256, 256), 256)
        asked = query[rows]
        scores_near = dot_t(asked, pair[:, 0:128])
        scores_far = dot_t(asked, pair_far[:, 0:128])
        top = jnp.maximum(
            jnp.max(scores_near, axis=1, keepdims=True), jnp.max(scores_far, axis=1, keepdims=True)
        )
        shifted_near = jnp.exp((scores_near - top) * scale)
        shifted_far = jnp.exp((scores_far - top) * scale)
        total = jnp.sum(shifted_near, axis=1, keepdims=True) + jnp.sum(
            shifted_far, axis=1, keepdims=True
        )
        attended = dot(shifted_near.astype(BF), pair[:, 128:256])
        attended = attended + dot(shifted_far.astype(BF), pair_far[:, 128:256])
        attended = (attended / total).astype(BF)
        terms = dot(attended, head_out) + tokens[rows].astype(F32) * 0.0625
        for column in range(8):
            parts = [
                terms[y * 64 + column * 8 : y * 64 + column * 8 + 8] for y in range(4)
            ]
            terms_out[step * 8 + column] = jnp.concatenate(parts, 0).astype(BF)
        return 0

    lax.fori_loop(0, 4, one_block, 0)


def attend(query, pair, pair_far, tokens, near, far):
    return pl.pallas_call(
        attend_kernel,
        out_shape=jax.ShapeDtypeStruct((32, 32, C), BF),
        cost_estimate=pl.CostEstimate(
            flops=2 * 1024 * 128 * (2 * 2048 + C),
            bytes_accessed=3_000_000,
            transcendentals=1024 * 2048,
        ),
        compiler_params=pltpu.CompilerParams(vmem_limit_bytes=24 << 20),
        name="attend",
    )(query, pair, pair_far, tokens, near, far)


def sum_kernel(terms, mixed_out):
    total = terms[0].astype(F32)
    for head in range(1, 16):
        total = total + terms[head].astype(F32)
    for half in range(2):
        for strip in range(8):
            part = total[half * 32 + strip * 4 : half * 32 + strip * 4 + 4].reshape(2, 2, C)
            at = strip * 4 + half * 2
            mixed_out[at : at + 2] = part.astype(BF)


def sum_heads(terms):
    return pl.pallas_call(
        sum_kernel,
        out_shape=jax.ShapeDtypeStruct((32, 2, C), BF),
        cost_estimate=pl.CostEstimate(
            flops=16 * 64 * C, bytes_accessed=700_000, transcendentals=0
        ),
        compiler_params=pltpu.CompilerParams(vmem_limit_bytes=8 << 20),
        name="sum_heads",
    )(terms)


def copy_kernel(source, target):
    target[...] = source[...]


def copied(array):
    return pl.pallas_call(
        copy_kernel,
        out_shape=jax.ShapeDtypeStruct(array.shape, array.dtype),
        compiler_params=pltpu.CompilerParams(vmem_limit_bytes=8 << 20),
        cost_estimate=pl.CostEstimate(flops=0, bytes_accessed=400_000, transcendentals=0),
        name="copied",
    )(array)


def nearest_plane(y, h, c, l):
    depth = 8 * h + l + 2 * y - 4 + c
    return l // 2, depth // 8, c, depth % 8


def plan(latent, conv_weight, conv_gain, qkv_weight, qk_gain, out_weight):
    core = lax.axis_index("c")
    first = core == 0
    core = core.astype(jnp.int32).reshape(1)
    tiles = exchange(latent, DEPTH)

    gains = qk_gain.reshape(2, 1, 64)
    gains = jnp.concatenate([jnp.pad(gains, ((0, 0), (0, 0), (0, 64))), jnp.pad(gains, ((0, 0), (0, 0), (64, 0)))], 1)
    gains = jnp.pad(gains.reshape(4, 128), ((0, 12), (0, C - 128)))
    packed = jnp.concatenate([qkv_weight.reshape(192, C), out_weight, gains], 0)
    near = move(packed, ("y", "h", "c", "l"), nearest_plane)
    far = swap(near)
    near, far = jnp.where(first, near, far), jnp.where(first, far, near)

    own = tiles.reshape(2, 8, 4, 4, C).transpose(1, 3, 0, 2, 4).reshape(32, 8, C)
    edge = move(
        jnp.where(first, own[:, 0:2], own[:, 6:8]), ("y", "c"), lambda y, c: (y - 1 + 2 * c, 1 - c)
    )
    other = swap(own)
    edge = edge.reshape(64, C)
    left, right = border(core, own, other, edge)
    before = move(right, ("x",), lambda x: (x + 1,))
    after = move(left, ("x",), lambda x: (x - 1,))

    feature_tiles, pooled = conv_stack(core, own, other, edge, before, after, conv_weight, conv_gain)

    tokens = exchange(pooled, ("x", "y")).reshape(1024, C)
    features = exchange(feature_tiles.reshape(16, 4, 4, C), DEPTH)

    query, pair = heads(tokens, near, far)
    pair_far = swap(pair)
    features = copied(features)
    terms = attend(query, pair, pair_far, tokens, near, far)
    terms = exchange(terms, PLANE)
    mixed = sum_heads(terms.reshape(16, 64, C))
    mixed = move(
        mixed,
        ("y", "h", "c", "x", "l"),
        lambda y, h, c, x, l: (2 * h + l // 4, (l // 2) % 2, l % 2, x, 2 * y + c),
    )
    return (features, mixed.reshape(1, 32, 2, C))


def solution(mesh):
    planes = Mesh(mesh.devices.reshape(tuple(SIZES.values())), tuple(SIZES))
    placed = (
        P(None, ROW, COL, None),
        P(),
        P(),
        P(None, COL, None),
        P(None, COL),
        P(COL, None),
    )
    return jax.shard_map(
        plan,
        mesh=planes,
        in_specs=placed,
        out_specs=(P(None, ROW, COL, None), P(ROW, None, COL, None)),
        check_vma=False,
    )
```

```python
import math

import jax
import jax.numpy as jnp
from jax import lax
from jax.experimental import pallas as pl
from jax.experimental.pallas import tpu as pltpu
from jax.sharding import Mesh
from jax.sharding import PartitionSpec as P


SIZES = {"y": 4, "h": 2, "c": 2, "x": 4, "l": 8}
ROW = ("y", "h", "c")
COL = ("x", "l")
DEPTH = ("h", "l")
PLANE = ("x", "y", "c")
C = 320
BF = jnp.bfloat16
F32 = jnp.float32


def move(array, axes, target):
    sizes = [SIZES[axis] for axis in axes]
    pairs = []
    count = 1
    for size in sizes:
        count *= size
    for index in range(count):
        rest, place = index, []
        for size in reversed(sizes):
            place.insert(0, rest % size)
            rest //= size
        flat = 0
        for size, value in zip(sizes, target(*place)):
            flat = flat * size + value % size
        pairs.append((index, flat))
    return lax.ppermute(array, axes, pairs)


def exchange(array, axes):
    return lax.all_to_all(array, axes, split_axis=0, concat_axis=0, tiled=True)


def swap(array):
    return lax.ppermute(array, "c", [(0, 1), (1, 0)])


def dot(left, right):
    return jnp.dot(left, right, preferred_element_type=F32)


def dot_t(left, right):
    return lax.dot_general(left, right, (((1,), (1,)), ((), ())), preferred_element_type=F32)


def picked(core, first, count, own, other, edge):
    place = lax.broadcasted_iota(jnp.int32, (count * 16, 1), 0)
    column = first + (place >> 4)
    row = ((place >> 3) & 1) * 8 + (place & 7) + core * 4 - 2
    local = column * 8 + ((row >> 3) & 1) * 4 + (row & 3)
    near = jnp.where(((row >> 2) & 1) == core, local, local + 256)
    source = jnp.where((row < 0) | (row > 15), 512 + column * 2 + (row & 1), near)
    at = lax.broadcasted_iota(jnp.int32, (count * 16, 576), 1)
    choice = (at == source).astype(F32).astype(BF)
    rows = dot(choice[:, 0:256], own[...].reshape(256, C))
    rows = rows + dot(choice[:, 256:512], other[...].reshape(256, C))
    return rows + dot(choice[:, 512:576], edge[...])


def border_kernel(core, own, other, edge, left_out, right_out):
    left_out[...] = picked(core[0], 0, 2, own, other, edge).astype(BF)
    right_out[...] = picked(core[0], 30, 2, own, other, edge).astype(BF)


def border(core, own, other, edge):
    return pl.pallas_call(
        border_kernel,
        out_shape=(jax.ShapeDtypeStruct((32, C), BF),) * 2,
        in_specs=[pl.BlockSpec(memory_space=pltpu.SMEM)] + [pl.BlockSpec(memory_space=pltpu.VMEM)] * 3,
        compiler_params=pltpu.CompilerParams(vmem_limit_bytes=8 << 20),
        cost_estimate=pl.CostEstimate(
            flops=2 * 64 * 576 * C, bytes_accessed=400_000, transcendentals=0
        ),
        name="border",
    )(core, own, other, edge)


def packed_rows(array, shift):
    pairs = array.reshape(array.shape[0] // 16, 2, 8, C)
    sub = lax.broadcasted_iota(jnp.int32, pairs[:, 0].shape, 1)
    upper = pltpu.roll(pairs[:, 0], (8 - shift) % 8, 1)
    lower = pltpu.roll(pairs[:, 1], 4 - shift, 1)
    return jnp.where(sub < 4, upper, lower).reshape(array.shape[0] // 2, C)


def conv_kernel(
    core,
    own,
    other,
    edge,
    before,
    after,
    stored_gains,
    stored,
    feat_out,
    pool_out,
    held,
    act,
    taps,
    taps_odd,
    gains,
    kernels,
    arrived,
    pool,
    sent,
):
    gain_fetch = pltpu.make_async_copy(stored_gains, gains, arrived.at[6])
    gain_fetch.start()
    fetches = []
    for layer in range(2):
        for b in range(3):
            fetch = pltpu.make_async_copy(
                stored.at[layer, :, b], kernels.at[layer, b], arrived.at[3 * layer + b]
            )
            fetch.start()
            fetches.append(fetch)

    def activation(wide, layer):
        factor = lax.rsqrt(jnp.mean(wide * wide, axis=-1, keepdims=True) + 1e-06)
        scaled = wide * factor * gains[layer : layer + 1]
        return scaled * jax.nn.sigmoid(scaled)

    def tap(rows, layer, b):
        fetches[3 * layer + b].wait()
        return dot(rows, kernels[layer, b].reshape(3 * C, C))

    held[0:32] = before[...].astype(F32)
    held[32:544] = picked(core[0], 0, 32, own, other, edge)
    held[544:576] = after[...].astype(F32)
    gain_fetch.wait()
    act[0:576] = activation(held[0:576], 0)
    act[576:592] = jnp.zeros((16, C), F32)
    for a in range(3):
        taps[:, a * C : (a + 1) * C] = act[a : a + 576].astype(BF)
    total = tap(taps[0:544], 0, 0) + tap(taps[16:560], 0, 1) + tap(taps[32:576], 0, 2)
    held[576:592] = jnp.zeros((16, C), F32)
    middle = (held[17:561] + total).astype(BF).astype(F32)
    center = packed_rows(middle, 1)[8:264]
    wide = activation(middle, 1)
    for a in range(3):
        rows = packed_rows(wide, a)
        taps[0:272, a * C : (a + 1) * C] = rows.astype(BF)
        taps_odd[:, a * C : (a + 1) * C] = rows[8:264].astype(BF)
    total = tap(taps[0:256], 1, 0) + tap(taps_odd[...], 1, 1) + tap(taps[16:272], 1, 2)
    fresh = (center + total).astype(BF)
    place = lax.broadcasted_iota(jnp.int32, (64, 256), 1)
    index = lax.broadcasted_iota(jnp.int32, (64, 256), 0)
    same = ((place >> 4) == (index >> 3) * 2 + (index & 1)) & (
        ((place >> 1) & 3) == ((index >> 2) & 1) * 2 + ((index >> 1) & 1)
    )
    pooled = dot(jnp.where(same, 0.25, 0.0).astype(BF), fresh).astype(BF)
    pool[...] = pooled
    copies = [pltpu.make_async_copy(pool, pool_out.at[slot], sent.at[slot]) for slot in range(16)]
    for copy in copies:
        copy.start()
    place = lax.broadcasted_iota(jnp.int32, (256, 256), 1)
    index = lax.broadcasted_iota(jnp.int32, (256, 256), 0)
    source = (((index >> 4) & 7) * 4 + (index & 3)) * 8 + (index >> 7) * 4 + ((index >> 2) & 3)
    feat_out[...] = dot((place == source).astype(F32).astype(BF), fresh).astype(BF)
    for copy in copies:
        copy.wait()


def conv_stack(core, own, other, edge, before, after, kernels, gains):
    return pl.pallas_call(
        conv_kernel,
        out_shape=(
            jax.ShapeDtypeStruct((256, C), BF),
            jax.ShapeDtypeStruct((16, 64, C), BF),
        ),
        out_specs=(pl.BlockSpec(memory_space=pltpu.VMEM), pl.BlockSpec(memory_space=pltpu.HBM)),
        in_specs=[pl.BlockSpec(memory_space=pltpu.SMEM)]
        + [pl.BlockSpec(memory_space=pltpu.VMEM)] * 5
        + [pl.BlockSpec(memory_space=pltpu.HBM)] * 2,
        scratch_shapes=[
            pltpu.VMEM((608, C), F32),
            pltpu.VMEM((608, C), F32),
            pltpu.VMEM((576, 3 * C), BF),
            pltpu.VMEM((256, 3 * C), BF),
            pltpu.VMEM((2, C), F32),
            pltpu.VMEM((2, 3, 3, C, C), BF),
            pltpu.SemaphoreType.DMA((7,)),
            pltpu.VMEM((64, C), BF),
            pltpu.SemaphoreType.DMA((16,)),
        ],
        cost_estimate=pl.CostEstimate(
            flops=2 * 1056 * 9 * C * C, bytes_accessed=5_000_000, transcendentals=360_000
        ),
        compiler_params=pltpu.CompilerParams(vmem_limit_bytes=52 << 20),
        name="conv_stack",
    )(core, own, other, edge, before, after, gains, kernels)


def norm(projected, gain):
    factor = lax.rsqrt(jnp.mean(projected * projected, axis=-1, keepdims=True) + 1e-06)
    return (projected * factor * gain).astype(BF)


def heads_kernel(tokens, near, far, query_out, pair_out):
    def both(start):
        return jnp.concatenate([near[start : start + 64], far[start : start + 64]], 0)

    matrix = jnp.concatenate([both(0), both(64), both(128)], 0)
    projected = dot_t(tokens[...], matrix)
    query_gain = near[256:257, 0:128].astype(F32) + far[257:258, 0:128].astype(F32)
    key_gain = near[258:259, 0:128].astype(F32) + far[259:260, 0:128].astype(F32)
    query_out[...] = norm(projected[:, 0:128], query_gain * (128 ** (-0.5) * math.log2(math.e)))
    pair_out[:, 0:128] = norm(projected[:, 128:256], key_gain)
    pair_out[:, 128:256] = projected[:, 256:384].astype(BF)


def heads(tokens, near, far):
    return pl.pallas_call(
        heads_kernel,
        out_shape=(
            jax.ShapeDtypeStruct((1024, 128), BF),
            jax.ShapeDtypeStruct((1024, 256), BF),
        ),
        cost_estimate=pl.CostEstimate(
            flops=2 * 1024 * 384 * C, bytes_accessed=2_000_000, transcendentals=2048
        ),
        compiler_params=pltpu.CompilerParams(vmem_limit_bytes=16 << 20),
        name="heads",
    )(tokens, near, far)


def attend_kernel(query, pair, pair_far, tokens, near, far, terms_out, ready, sent):
    head_out = jnp.concatenate([near[192:256], far[192:256]], 0)

    def send(step):
        part = pl.ds(pl.multiple_of(step * 8, 8), 8)
        return pltpu.make_async_copy(ready.at[part], terms_out.at[part], sent.at[step])

    def one_block(step, _):
        rows = pl.ds(pl.multiple_of(step * 256, 256), 256)
        asked = query[rows]
        scores = dot_t(asked, pair[:, 0:128])
        scores_far = dot_t(asked, pair_far[:, 0:128])
        top = jnp.maximum(
            jnp.max(scores, axis=1, keepdims=True), jnp.max(scores_far, axis=1, keepdims=True)
        )
        shifted = jnp.exp2(scores - top)
        shifted_far = jnp.exp2(scores_far - top)
        total = jnp.sum(shifted, axis=1, keepdims=True) + jnp.sum(shifted_far, axis=1, keepdims=True)
        attended = dot(shifted.astype(BF), pair[:, 128:256])
        attended = attended + dot(shifted_far.astype(BF), pair_far[:, 128:256])
        attended = (attended / total).astype(BF)
        terms = dot(attended, head_out) + tokens[rows].astype(F32) * 0.0625
        for column in range(8):
            parts = [
                terms[y * 64 + column * 8 : y * 64 + column * 8 + 8] for y in range(4)
            ]
            ready[step * 8 + column] = jnp.concatenate(parts, 0).astype(BF)
        send(step).start()
        return 0

    lax.fori_loop(0, 4, one_block, 0, unroll=True)
    for step in range(4):
        send(step).wait()


def attend(query, pair, pair_far, tokens, near, far):
    return pl.pallas_call(
        attend_kernel,
        out_shape=jax.ShapeDtypeStruct((32, 32, C), BF),
        out_specs=pl.BlockSpec(memory_space=pltpu.HBM),
        scratch_shapes=[pltpu.VMEM((32, 32, C), BF), pltpu.SemaphoreType.DMA((4,))],
        cost_estimate=pl.CostEstimate(
            flops=2 * 1024 * 128 * (2 * 2048 + C),
            bytes_accessed=3_000_000,
            transcendentals=1024 * 2048,
        ),
        compiler_params=pltpu.CompilerParams(vmem_limit_bytes=24 << 20),
        name="attend",
    )(query, pair, pair_far, tokens, near, far)


def sum_kernel(terms, mixed_out):
    total = terms[0].astype(F32)
    for head in range(1, 16):
        total = total + terms[head].astype(F32)
    for half in range(2):
        for strip in range(8):
            part = total[half * 32 + strip * 4 : half * 32 + strip * 4 + 4].reshape(2, 2, C)
            at = strip * 4 + half * 2
            mixed_out[at : at + 2] = part.astype(BF)


def sum_heads(terms):
    return pl.pallas_call(
        sum_kernel,
        out_shape=jax.ShapeDtypeStruct((32, 2, C), BF),
        cost_estimate=pl.CostEstimate(
            flops=16 * 64 * C, bytes_accessed=700_000, transcendentals=0
        ),
        compiler_params=pltpu.CompilerParams(vmem_limit_bytes=8 << 20),
        name="sum_heads",
    )(terms)


def copy_kernel(source, target):
    target[...] = source[...]


def copied(array):
    return pl.pallas_call(
        copy_kernel,
        out_shape=jax.ShapeDtypeStruct(array.shape, array.dtype),
        compiler_params=pltpu.CompilerParams(vmem_limit_bytes=8 << 20),
        cost_estimate=pl.CostEstimate(flops=0, bytes_accessed=400_000, transcendentals=0),
        name="copied",
    )(array)


def nearest_plane(y, h, c, l):
    depth = 8 * h + l + 2 * y - 4 + c
    return l // 2, depth // 8, c, depth % 8


def plan(latent, conv_weight, conv_gain, qkv_weight, qk_gain, out_weight):
    core = lax.axis_index("c")
    first = core == 0
    core = core.astype(jnp.int32).reshape(1)
    tiles = exchange(latent, DEPTH)

    gains = qk_gain.reshape(2, 1, 64)
    gains = jnp.concatenate([jnp.pad(gains, ((0, 0), (0, 0), (0, 64))), jnp.pad(gains, ((0, 0), (0, 0), (64, 0)))], 1)
    gains = jnp.pad(gains.reshape(4, 128), ((0, 12), (0, C - 128)))
    packed = jnp.concatenate([qkv_weight.reshape(192, C), out_weight, gains], 0)
    near = move(packed, ("y", "h", "c", "l"), nearest_plane)
    far = swap(near)
    near, far = jnp.where(first, near, far), jnp.where(first, far, near)

    own = tiles.reshape(2, 8, 4, 4, C).transpose(1, 3, 0, 2, 4).reshape(32, 8, C)
    edge = move(
        jnp.where(first, own[:, 0:2], own[:, 6:8]), ("y", "c"), lambda y, c: (y - 1 + 2 * c, 1 - c)
    )
    other = swap(own)
    edge = edge.reshape(64, C)
    left, right = border(core, own, other, edge)
    before = move(right, ("x",), lambda x: (x + 1,))
    after = move(left, ("x",), lambda x: (x - 1,))

    feature_tiles, pooled = conv_stack(core, own, other, edge, before, after, conv_weight, conv_gain)

    tokens = exchange(pooled, ("x", "y")).reshape(1024, C)
    features = exchange(feature_tiles.reshape(16, 4, 4, C), DEPTH)

    query, pair = heads(tokens, near, far)
    pair_far = swap(pair)
    features = copied(features)
    terms = attend(query, pair, pair_far, tokens, near, far)
    terms = exchange(terms, PLANE)
    mixed = sum_heads(terms.reshape(16, 64, C))
    mixed = move(
        mixed,
        ("y", "h", "c", "x", "l"),
        lambda y, h, c, x, l: (2 * h + l // 4, (l // 2) % 2, l % 2, x, 2 * y + c),
    )
    return (features, mixed.reshape(1, 32, 2, C))


def solution(mesh):
    planes = Mesh(mesh.devices.reshape(tuple(SIZES.values())), tuple(SIZES))
    placed = (
        P(None, ROW, COL, None),
        P(),
        P(),
        P(None, COL, None),
        P(None, COL),
        P(COL, None),
    )
    return jax.shard_map(
        plan,
        mesh=planes,
        in_specs=placed,
        out_specs=(P(None, ROW, COL, None), P(ROW, None, COL, None)),
        check_vma=False,
    )
```

```python
import math

import jax
import jax.numpy as jnp
from jax import lax
from jax.experimental import pallas as pl
from jax.experimental.pallas import tpu as pltpu
from jax.sharding import Mesh
from jax.sharding import PartitionSpec as P


SIZES = {"y": 4, "h": 2, "c": 2, "x": 4, "l": 8}
ROW = ("y", "h", "c")
COL = ("x", "l")
DEPTH = ("h", "l")
PLANE = ("x", "y", "c")
C = 320
BF = jnp.bfloat16
F32 = jnp.float32


def move(array, axes, target):
    sizes = [SIZES[axis] for axis in axes]
    pairs = []
    count = 1
    for size in sizes:
        count *= size
    for index in range(count):
        rest, place = index, []
        for size in reversed(sizes):
            place.insert(0, rest % size)
            rest //= size
        flat = 0
        for size, value in zip(sizes, target(*place)):
            flat = flat * size + value % size
        pairs.append((index, flat))
    return lax.ppermute(array, axes, pairs)


def exchange(array, axes):
    return lax.all_to_all(array, axes, split_axis=0, concat_axis=0, tiled=True)


def swap(array):
    return lax.ppermute(array, "c", [(0, 1), (1, 0)])


def dot(left, right):
    return jnp.dot(left, right, preferred_element_type=F32)


def dot_t(left, right):
    return lax.dot_general(left, right, (((1,), (1,)), ((), ())), preferred_element_type=F32)


def picked(core, first, count, own, other, edge):
    place = lax.broadcasted_iota(jnp.int32, (count * 16, 1), 0)
    column = first + (place >> 4)
    row = ((place >> 3) & 1) * 8 + (place & 7) + core * 4 - 2
    local = column * 8 + ((row >> 3) & 1) * 4 + (row & 3)
    near = jnp.where(((row >> 2) & 1) == core, local, local + 256)
    source = jnp.where((row < 0) | (row > 15), 512 + column * 2 + (row & 1), near)
    at = lax.broadcasted_iota(jnp.int32, (count * 16, 576), 1)
    choice = (at == source).astype(F32).astype(BF)
    rows = dot(choice[:, 0:256], own[...].reshape(256, C))
    rows = rows + dot(choice[:, 256:512], other[...].reshape(256, C))
    return rows + dot(choice[:, 512:576], edge[...])


def border_kernel(core, own, other, edge, left_out, right_out):
    left_out[...] = picked(core[0], 0, 2, own, other, edge).astype(BF)
    right_out[...] = picked(core[0], 30, 2, own, other, edge).astype(BF)


def border(core, own, other, edge):
    return pl.pallas_call(
        border_kernel,
        out_shape=(jax.ShapeDtypeStruct((32, C), BF),) * 2,
        in_specs=[pl.BlockSpec(memory_space=pltpu.SMEM)] + [pl.BlockSpec(memory_space=pltpu.VMEM)] * 3,
        compiler_params=pltpu.CompilerParams(vmem_limit_bytes=8 << 20),
        cost_estimate=pl.CostEstimate(
            flops=2 * 64 * 576 * C, bytes_accessed=400_000, transcendentals=0
        ),
        name="border",
    )(core, own, other, edge)


def packed_rows(array, shift):
    pairs = array.reshape(array.shape[0] // 16, 2, 8, C)
    sub = lax.broadcasted_iota(jnp.int32, pairs[:, 0].shape, 1)
    upper = pltpu.roll(pairs[:, 0], (8 - shift) % 8, 1)
    lower = pltpu.roll(pairs[:, 1], 4 - shift, 1)
    return jnp.where(sub < 4, upper, lower).reshape(array.shape[0] // 2, C)


def conv_kernel(
    core,
    own,
    other,
    edge,
    before,
    after,
    gains,
    stored,
    feat_out,
    pool_out,
    held,
    act,
    taps,
    taps_odd,
    kernels,
    arrived,
    pool,
    sent,
):
    fetches = []
    for layer in range(2):
        for b in range(3):
            fetch = pltpu.make_async_copy(
                stored.at[layer, :, b], kernels.at[layer, b], arrived.at[3 * layer + b]
            )
            fetch.start()
            fetches.append(fetch)

    def activation(wide, layer):
        factor = lax.rsqrt(jnp.mean(wide * wide, axis=-1, keepdims=True) + 1e-06)
        scaled = wide * factor * gains[layer : layer + 1]
        return scaled * jax.nn.sigmoid(scaled)

    def tap(rows, layer, b):
        fetches[3 * layer + b].wait()
        return dot(rows, kernels[layer, b].reshape(3 * C, C))

    held[0:32] = before[...].astype(F32)
    held[32:544] = picked(core[0], 0, 32, own, other, edge)
    held[544:576] = after[...].astype(F32)
    act[0:576] = activation(held[0:576], 0)
    act[576:592] = jnp.zeros((16, C), F32)
    for a in range(3):
        taps[:, a * C : (a + 1) * C] = act[a : a + 576].astype(BF)
    total = tap(taps[0:544], 0, 0) + tap(taps[16:560], 0, 1) + tap(taps[32:576], 0, 2)
    held[576:592] = jnp.zeros((16, C), F32)
    middle = (held[17:561] + total).astype(BF).astype(F32)
    center = packed_rows(middle, 1)[8:264]
    wide = activation(middle, 1)
    for a in range(3):
        rows = packed_rows(wide, a)
        taps[0:272, a * C : (a + 1) * C] = rows.astype(BF)
        taps_odd[:, a * C : (a + 1) * C] = rows[8:264].astype(BF)
    total = tap(taps[0:256], 1, 0) + tap(taps_odd[...], 1, 1) + tap(taps[16:272], 1, 2)
    fresh = (center + total).astype(BF)
    place = lax.broadcasted_iota(jnp.int32, (64, 256), 1)
    index = lax.broadcasted_iota(jnp.int32, (64, 256), 0)
    same = ((place >> 4) == (index >> 3) * 2 + (index & 1)) & (
        ((place >> 1) & 3) == ((index >> 2) & 1) * 2 + ((index >> 1) & 1)
    )
    pooled = dot(jnp.where(same, 0.25, 0.0).astype(BF), fresh).astype(BF)
    pool[...] = pooled
    copies = [pltpu.make_async_copy(pool, pool_out.at[slot], sent.at[slot]) for slot in range(16)]
    for copy in copies:
        copy.start()
    place = lax.broadcasted_iota(jnp.int32, (256, 256), 1)
    index = lax.broadcasted_iota(jnp.int32, (256, 256), 0)
    source = (((index >> 4) & 7) * 4 + (index & 3)) * 8 + (index >> 7) * 4 + ((index >> 2) & 3)
    feat_out[...] = dot((place == source).astype(F32).astype(BF), fresh).astype(BF)
    for copy in copies:
        copy.wait()


def conv_stack(core, own, other, edge, before, after, kernels, gains):
    return pl.pallas_call(
        conv_kernel,
        out_shape=(
            jax.ShapeDtypeStruct((256, C), BF),
            jax.ShapeDtypeStruct((16, 64, C), BF),
        ),
        out_specs=(pl.BlockSpec(memory_space=pltpu.VMEM), pl.BlockSpec(memory_space=pltpu.HBM)),
        in_specs=[pl.BlockSpec(memory_space=pltpu.SMEM)]
        + [pl.BlockSpec(memory_space=pltpu.VMEM)] * 6
        + [pl.BlockSpec(memory_space=pltpu.HBM)],
        scratch_shapes=[
            pltpu.VMEM((608, C), F32),
            pltpu.VMEM((608, C), F32),
            pltpu.VMEM((576, 3 * C), BF),
            pltpu.VMEM((256, 3 * C), BF),
            pltpu.VMEM((2, 3, 3, C, C), BF),
            pltpu.SemaphoreType.DMA((6,)),
            pltpu.VMEM((64, C), BF),
            pltpu.SemaphoreType.DMA((16,)),
        ],
        cost_estimate=pl.CostEstimate(
            flops=2 * 1056 * 9 * C * C, bytes_accessed=5_000_000, transcendentals=360_000
        ),
        compiler_params=pltpu.CompilerParams(vmem_limit_bytes=52 << 20),
        name="conv_stack",
    )(core, own, other, edge, before, after, gains, kernels)


def norm(projected, gain):
    factor = lax.rsqrt(jnp.mean(projected * projected, axis=-1, keepdims=True) + 1e-06)
    return (projected * factor * gain).astype(BF)


def heads_kernel(tokens, near, far, query_out, pair_out):
    def both(start):
        return jnp.concatenate([near[start : start + 64], far[start : start + 64]], 0)

    matrix = jnp.concatenate([both(0), both(64), both(128)], 0)
    projected = dot_t(tokens[...], matrix)
    query_gain = near[256:257, 0:128].astype(F32) + far[257:258, 0:128].astype(F32)
    key_gain = near[258:259, 0:128].astype(F32) + far[259:260, 0:128].astype(F32)
    query_out[...] = norm(projected[:, 0:128], query_gain * (128 ** (-0.5) * math.log2(math.e)))
    pair_out[:, 0:128] = norm(projected[:, 128:256], key_gain)
    pair_out[:, 128:256] = projected[:, 256:384].astype(BF)


def heads(tokens, near, far):
    return pl.pallas_call(
        heads_kernel,
        out_shape=(
            jax.ShapeDtypeStruct((1024, 128), BF),
            jax.ShapeDtypeStruct((1024, 256), BF),
        ),
        cost_estimate=pl.CostEstimate(
            flops=2 * 1024 * 384 * C, bytes_accessed=2_000_000, transcendentals=2048
        ),
        compiler_params=pltpu.CompilerParams(vmem_limit_bytes=16 << 20),
        name="heads",
    )(tokens, near, far)


def attend_kernel(query, pair, pair_far, tokens, near, far, terms_out, ready, sent):
    head_out = jnp.concatenate([near[192:256], far[192:256]], 0)

    def send(step):
        part = pl.ds(pl.multiple_of(step * 8, 8), 8)
        return pltpu.make_async_copy(ready.at[part], terms_out.at[part], sent.at[step])

    def one_block(step, _):
        rows = pl.ds(pl.multiple_of(step * 256, 256), 256)
        asked = query[rows]
        scores = dot_t(asked, pair[:, 0:128])
        scores_far = dot_t(asked, pair_far[:, 0:128])
        top = jnp.maximum(
            jnp.max(scores, axis=1, keepdims=True), jnp.max(scores_far, axis=1, keepdims=True)
        )
        shifted = jnp.exp2(scores - top)
        shifted_far = jnp.exp2(scores_far - top)
        total = jnp.sum(shifted, axis=1, keepdims=True) + jnp.sum(shifted_far, axis=1, keepdims=True)
        attended = dot(shifted.astype(BF), pair[:, 128:256])
        attended = attended + dot(shifted_far.astype(BF), pair_far[:, 128:256])
        attended = (attended / total).astype(BF)
        terms = dot(attended, head_out) + tokens[rows].astype(F32) * 0.0625
        for column in range(8):
            parts = [
                terms[y * 64 + column * 8 : y * 64 + column * 8 + 8] for y in range(4)
            ]
            ready[step * 8 + column] = jnp.concatenate(parts, 0).astype(BF)
        send(step).start()
        return 0

    lax.fori_loop(0, 4, one_block, 0, unroll=True)
    for step in range(4):
        send(step).wait()


def attend(query, pair, pair_far, tokens, near, far):
    return pl.pallas_call(
        attend_kernel,
        out_shape=jax.ShapeDtypeStruct((32, 32, C), BF),
        out_specs=pl.BlockSpec(memory_space=pltpu.HBM),
        scratch_shapes=[pltpu.VMEM((32, 32, C), BF), pltpu.SemaphoreType.DMA((4,))],
        cost_estimate=pl.CostEstimate(
            flops=2 * 1024 * 128 * (2 * 2048 + C),
            bytes_accessed=3_000_000,
            transcendentals=1024 * 2048,
        ),
        compiler_params=pltpu.CompilerParams(vmem_limit_bytes=24 << 20),
        name="attend",
    )(query, pair, pair_far, tokens, near, far)


def sum_kernel(terms, mixed_out):
    total = terms[0].astype(F32)
    for head in range(1, 16):
        total = total + terms[head].astype(F32)
    for half in range(2):
        for strip in range(8):
            part = total[half * 32 + strip * 4 : half * 32 + strip * 4 + 4].reshape(2, 2, C)
            at = strip * 4 + half * 2
            mixed_out[at : at + 2] = part.astype(BF)


def sum_heads(terms):
    return pl.pallas_call(
        sum_kernel,
        out_shape=jax.ShapeDtypeStruct((32, 2, C), BF),
        cost_estimate=pl.CostEstimate(
            flops=16 * 64 * C, bytes_accessed=700_000, transcendentals=0
        ),
        compiler_params=pltpu.CompilerParams(vmem_limit_bytes=8 << 20),
        name="sum_heads",
    )(terms)


def copy_kernel(source, target):
    target[...] = source[...]


def copied(array):
    return pl.pallas_call(
        copy_kernel,
        out_shape=jax.ShapeDtypeStruct(array.shape, array.dtype),
        compiler_params=pltpu.CompilerParams(vmem_limit_bytes=8 << 20),
        cost_estimate=pl.CostEstimate(flops=0, bytes_accessed=400_000, transcendentals=0),
        name="copied",
    )(array)


def nearest_plane(y, h, c, l):
    depth = 8 * h + l + 2 * y - 4 + c
    return l // 2, depth // 8, c, depth % 8


def plan(latent, conv_weight, conv_gain, qkv_weight, qk_gain, out_weight):
    core = lax.axis_index("c")
    first = core == 0
    core = core.astype(jnp.int32).reshape(1)
    near = move(qkv_weight.reshape(192, C), ("y", "h", "c", "l"), nearest_plane)

    tiles = exchange(latent, DEPTH)

    gains = qk_gain.reshape(2, 1, 64)
    gains = jnp.concatenate(
        [jnp.pad(gains, ((0, 0), (0, 0), (0, 64))), jnp.pad(gains, ((0, 0), (0, 0), (64, 0)))], 1
    )
    gains = jnp.pad(gains.reshape(4, 128), ((0, 12), (0, C - 128)))
    rest = move(
        jnp.concatenate([out_weight, gains], 0), ("y", "h", "c", "l"), nearest_plane
    )
    near = jnp.concatenate([near, rest], 0)
    conv_gain = jnp.pad(conv_gain, ((0, 6), (0, 0)))
    far = swap(near)
    near, far = jnp.where(first, near, far), jnp.where(first, far, near)

    own = tiles.reshape(2, 8, 4, 4, C).transpose(1, 3, 0, 2, 4).reshape(32, 8, C)
    edge = move(
        jnp.where(first, own[:, 0:2], own[:, 6:8]), ("y", "c"), lambda y, c: (y - 1 + 2 * c, 1 - c)
    )
    other = swap(own)
    edge = edge.reshape(64, C)
    left, right = border(core, own, other, edge)
    before = move(right, ("x",), lambda x: (x + 1,))
    after = move(left, ("x",), lambda x: (x - 1,))

    feature_tiles, pooled = conv_stack(core, own, other, edge, before, after, conv_weight, conv_gain)

    tokens = exchange(pooled, ("x", "y")).reshape(1024, C)
    features = exchange(feature_tiles.reshape(16, 4, 4, C), DEPTH)

    query, pair = heads(tokens, near, far)
    pair_far = swap(pair)
    features = copied(features)
    terms = attend(query, pair, pair_far, tokens, near, far)
    terms = exchange(terms, PLANE)
    mixed = sum_heads(terms.reshape(16, 64, C))
    mixed = move(
        mixed,
        ("y", "h", "c", "x", "l"),
        lambda y, h, c, x, l: (2 * h + l // 4, (l // 2) % 2, l % 2, x, 2 * y + c),
    )
    return (features, mixed.reshape(1, 32, 2, C))


def solution(mesh):
    planes = Mesh(mesh.devices.reshape(tuple(SIZES.values())), tuple(SIZES))
    placed = (
        P(None, ROW, COL, None),
        P(),
        P(),
        P(None, COL, None),
        P(None, COL),
        P(COL, None),
    )
    return jax.shard_map(
        plan,
        mesh=planes,
        in_specs=placed,
        out_specs=(P(None, ROW, COL, None), P(ROW, None, COL, None)),
        check_vma=False,
    )
```

```python
import math

import jax
import jax.numpy as jnp
from jax import lax
from jax.experimental import pallas as pl
from jax.experimental.pallas import tpu as pltpu
from jax.sharding import Mesh
from jax.sharding import PartitionSpec as P


SIZES = {"y": 4, "h": 2, "c": 2, "x": 4, "l": 8}
ROW = ("y", "h", "c")
COL = ("x", "l")
DEPTH = ("h", "l")
PLANE = ("x", "y", "c")
C = 320
BF = jnp.bfloat16
F32 = jnp.float32


def move(array, axes, target):
    sizes = [SIZES[axis] for axis in axes]
    pairs = []
    count = 1
    for size in sizes:
        count *= size
    for index in range(count):
        rest, place = index, []
        for size in reversed(sizes):
            place.insert(0, rest % size)
            rest //= size
        flat = 0
        for size, value in zip(sizes, target(*place)):
            flat = flat * size + value % size
        pairs.append((index, flat))
    return lax.ppermute(array, axes, pairs)


def exchange(array, axes):
    return lax.all_to_all(array, axes, split_axis=0, concat_axis=0, tiled=True)


def swap(array):
    return lax.ppermute(array, "c", [(0, 1), (1, 0)])


def dot(left, right):
    return jnp.dot(left, right, preferred_element_type=F32)


def dot_t(left, right):
    return lax.dot_general(left, right, (((1,), (1,)), ((), ())), preferred_element_type=F32)


def dense(array):
    half = array.shape[-2] // 2
    tail = array[..., 256:C]
    tail = jnp.concatenate([tail[..., 0:half, :], tail[..., half:, :]], -1)
    return jnp.concatenate([array[..., 0:128], array[..., 128:256], tail], -2)


def undense(array):
    rows = array.shape[-2] * 2 // 5
    tail = array[..., 2 * rows :, :]
    tail = jnp.concatenate([tail[..., 0:64], tail[..., 64:128]], -2)
    return jnp.concatenate([array[..., 0:rows, :], array[..., rows : 2 * rows, :], tail], -1)


def picked(core, first, count, own, other, edge):
    place = lax.broadcasted_iota(jnp.int32, (count * 16, 1), 0)
    column = first + (place >> 4)
    row = ((place >> 3) & 1) * 8 + (place & 7) + core * 4 - 2
    local = column * 8 + ((row >> 3) & 1) * 4 + (row & 3)
    near = jnp.where(((row >> 2) & 1) == core, local, local + 256)
    source = jnp.where((row < 0) | (row > 15), 512 + column * 2 + (row & 1), near)
    at = lax.broadcasted_iota(jnp.int32, (count * 16, 576), 1)
    choice = (at == source).astype(F32).astype(BF)
    rows = dot(choice[:, 0:256], own[...].reshape(256, C))
    rows = rows + dot(choice[:, 256:512], other[...].reshape(256, C))
    return rows + dot(choice[:, 512:576], edge[...])


def border_kernel(core, own, other, edge, left_out, right_out):
    left_out[...] = picked(core[0], 0, 2, own, other, edge).astype(BF)
    right_out[...] = picked(core[0], 30, 2, own, other, edge).astype(BF)


def border(core, own, other, edge):
    return pl.pallas_call(
        border_kernel,
        out_shape=(jax.ShapeDtypeStruct((32, C), BF),) * 2,
        in_specs=[pl.BlockSpec(memory_space=pltpu.SMEM)] + [pl.BlockSpec(memory_space=pltpu.VMEM)] * 3,
        compiler_params=pltpu.CompilerParams(vmem_limit_bytes=8 << 20),
        cost_estimate=pl.CostEstimate(
            flops=2 * 64 * 576 * C, bytes_accessed=400_000, transcendentals=0
        ),
        name="border",
    )(core, own, other, edge)


def packed_rows(array, shift):
    pairs = array.reshape(array.shape[0] // 16, 2, 8, C)
    sub = lax.broadcasted_iota(jnp.int32, pairs[:, 0].shape, 1)
    upper = pltpu.roll(pairs[:, 0], (8 - shift) % 8, 1)
    lower = pltpu.roll(pairs[:, 1], 4 - shift, 1)
    return jnp.where(sub < 4, upper, lower).reshape(array.shape[0] // 2, C)


def conv_kernel(
    core,
    own,
    other,
    edge,
    before,
    after,
    gains,
    stored,
    feat_out,
    pool_out,
    held,
    act,
    taps,
    taps_odd,
    kernels,
    arrived,
    pool,
    sent,
):
    fetches = []
    for layer in range(2):
        for b in range(3):
            fetch = pltpu.make_async_copy(
                stored.at[layer, :, b], kernels.at[layer, b], arrived.at[3 * layer + b]
            )
            fetch.start()
            fetches.append(fetch)

    def activation(wide, layer):
        factor = lax.rsqrt(jnp.mean(wide * wide, axis=-1, keepdims=True) + 1e-06)
        scaled = wide * factor * gains[layer : layer + 1]
        return scaled * jax.nn.sigmoid(scaled)

    def tap(rows, layer, b):
        fetches[3 * layer + b].wait()
        return dot(rows, kernels[layer, b].reshape(3 * C, C))

    held[0:32] = before[...].astype(F32)
    held[32:544] = picked(core[0], 0, 32, own, other, edge)
    held[544:576] = after[...].astype(F32)
    act[0:576] = activation(held[0:576], 0)
    act[576:592] = jnp.zeros((16, C), F32)
    for a in range(3):
        taps[:, a * C : (a + 1) * C] = act[a : a + 576].astype(BF)
    total = tap(taps[0:544], 0, 0) + tap(taps[16:560], 0, 1) + tap(taps[32:576], 0, 2)
    held[576:592] = jnp.zeros((16, C), F32)
    middle = (held[17:561] + total).astype(BF).astype(F32)
    center = packed_rows(middle, 1)[8:264]
    wide = activation(middle, 1)
    for a in range(3):
        rows = packed_rows(wide, a)
        taps[0:272, a * C : (a + 1) * C] = rows.astype(BF)
        taps_odd[:, a * C : (a + 1) * C] = rows[8:264].astype(BF)
    total = tap(taps[0:256], 1, 0) + tap(taps_odd[...], 1, 1) + tap(taps[16:272], 1, 2)
    fresh = (center + total).astype(BF)
    place = lax.broadcasted_iota(jnp.int32, (64, 256), 1)
    index = lax.broadcasted_iota(jnp.int32, (64, 256), 0)
    same = ((place >> 4) == (index >> 3) * 2 + (index & 1)) & (
        ((place >> 1) & 3) == ((index >> 2) & 1) * 2 + ((index >> 1) & 1)
    )
    pooled = dot(jnp.where(same, 0.25, 0.0).astype(BF), fresh).astype(BF)
    pool[...] = pooled
    copies = [pltpu.make_async_copy(pool, pool_out.at[slot], sent.at[slot]) for slot in range(16)]
    for copy in copies:
        copy.start()
    place = lax.broadcasted_iota(jnp.int32, (256, 256), 1)
    index = lax.broadcasted_iota(jnp.int32, (256, 256), 0)
    source = (((index >> 4) & 7) * 4 + (index & 3)) * 8 + (index >> 7) * 4 + ((index >> 2) & 3)
    tiles = dot((place == source).astype(F32).astype(BF), fresh).reshape(16, 16, C)
    feat_out[...] = dense(tiles).astype(BF)
    for copy in copies:
        copy.wait()


def conv_stack(core, own, other, edge, before, after, kernels, gains):
    return pl.pallas_call(
        conv_kernel,
        out_shape=(
            jax.ShapeDtypeStruct((16, 40, 128), BF),
            jax.ShapeDtypeStruct((16, 64, C), BF),
        ),
        out_specs=(pl.BlockSpec(memory_space=pltpu.VMEM), pl.BlockSpec(memory_space=pltpu.HBM)),
        in_specs=[pl.BlockSpec(memory_space=pltpu.SMEM)]
        + [pl.BlockSpec(memory_space=pltpu.VMEM)] * 6
        + [pl.BlockSpec(memory_space=pltpu.HBM)],
        scratch_shapes=[
            pltpu.VMEM((608, C), F32),
            pltpu.VMEM((608, C), F32),
            pltpu.VMEM((576, 3 * C), BF),
            pltpu.VMEM((256, 3 * C), BF),
            pltpu.VMEM((2, 3, 3, C, C), BF),
            pltpu.SemaphoreType.DMA((6,)),
            pltpu.VMEM((64, C), BF),
            pltpu.SemaphoreType.DMA((16,)),
        ],
        cost_estimate=pl.CostEstimate(
            flops=2 * 1056 * 9 * C * C, bytes_accessed=5_000_000, transcendentals=360_000
        ),
        compiler_params=pltpu.CompilerParams(vmem_limit_bytes=52 << 20),
        name="conv_stack",
    )(core, own, other, edge, before, after, gains, kernels)


def norm(projected, gain):
    factor = lax.rsqrt(jnp.mean(projected * projected, axis=-1, keepdims=True) + 1e-06)
    return (projected * factor * gain).astype(BF)


def heads_kernel(tokens, near, far, query_out, pair_out):
    def both(start):
        return jnp.concatenate([near[start : start + 64], far[start : start + 64]], 0)

    matrix = jnp.concatenate([both(0), both(64), both(128)], 0)
    projected = dot_t(tokens[...], matrix)
    query_gain = near[256:257, 0:128].astype(F32) + far[257:258, 0:128].astype(F32)
    key_gain = near[258:259, 0:128].astype(F32) + far[259:260, 0:128].astype(F32)
    query_out[...] = norm(projected[:, 0:128], query_gain * (128 ** (-0.5) * math.log2(math.e)))
    pair_out[:, 0:128] = norm(projected[:, 128:256], key_gain)
    pair_out[:, 128:256] = projected[:, 256:384].astype(BF)


def heads(tokens, near, far):
    return pl.pallas_call(
        heads_kernel,
        out_shape=(
            jax.ShapeDtypeStruct((1024, 128), BF),
            jax.ShapeDtypeStruct((1024, 256), BF),
        ),
        cost_estimate=pl.CostEstimate(
            flops=2 * 1024 * 384 * C, bytes_accessed=2_000_000, transcendentals=2048
        ),
        compiler_params=pltpu.CompilerParams(vmem_limit_bytes=16 << 20),
        name="heads",
    )(tokens, near, far)


def attend_kernel(query, pair, pair_far, tokens, near, far, terms_out, ready, sent):
    head_out = jnp.concatenate([near[192:256], far[192:256]], 0)

    def send(step):
        part = pl.ds(pl.multiple_of(step * 8, 8), 8)
        return pltpu.make_async_copy(ready.at[part], terms_out.at[part], sent.at[step])

    def one_block(step, _):
        rows = pl.ds(pl.multiple_of(step * 256, 256), 256)
        asked = query[rows]
        scores = dot_t(asked, pair[:, 0:128])
        scores_far = dot_t(asked, pair_far[:, 0:128])
        top = jnp.maximum(
            jnp.max(scores, axis=1, keepdims=True), jnp.max(scores_far, axis=1, keepdims=True)
        )
        shifted = jnp.exp2(scores - top)
        shifted_far = jnp.exp2(scores_far - top)
        total = jnp.sum(shifted, axis=1, keepdims=True) + jnp.sum(shifted_far, axis=1, keepdims=True)
        attended = dot(shifted.astype(BF), pair[:, 128:256])
        attended = attended + dot(shifted_far.astype(BF), pair_far[:, 128:256])
        attended = (attended / total).astype(BF)
        terms = dot(attended, head_out) + tokens[rows].astype(F32) * 0.0625
        for column in range(8):
            parts = [
                terms[y * 64 + column * 8 : y * 64 + column * 8 + 8] for y in range(4)
            ]
            ready[step * 8 + column] = dense(jnp.concatenate(parts, 0)).astype(BF)
        send(step).start()
        return 0

    lax.fori_loop(0, 4, one_block, 0, unroll=True)
    for step in range(4):
        send(step).wait()


def attend(query, pair, pair_far, tokens, near, far):
    return pl.pallas_call(
        attend_kernel,
        out_shape=jax.ShapeDtypeStruct((32, 80, 128), BF),
        out_specs=pl.BlockSpec(memory_space=pltpu.HBM),
        scratch_shapes=[pltpu.VMEM((32, 80, 128), BF), pltpu.SemaphoreType.DMA((4,))],
        cost_estimate=pl.CostEstimate(
            flops=2 * 1024 * 128 * (2 * 2048 + C),
            bytes_accessed=3_000_000,
            transcendentals=1024 * 2048,
        ),
        compiler_params=pltpu.CompilerParams(vmem_limit_bytes=24 << 20),
        name="attend",
    )(query, pair, pair_far, tokens, near, far)


def sum_kernel(terms, mixed_out):
    total = terms[0:2].astype(F32)
    for head in range(1, 16):
        total = total + terms[2 * head : 2 * head + 2].astype(F32)
    total = undense(total).reshape(64, C)
    for half in range(2):
        for strip in range(8):
            part = total[half * 32 + strip * 4 : half * 32 + strip * 4 + 4].reshape(2, 2, C)
            at = strip * 4 + half * 2
            mixed_out[at : at + 2] = part.astype(BF)


def sum_heads(terms):
    return pl.pallas_call(
        sum_kernel,
        out_shape=jax.ShapeDtypeStruct((32, 2, C), BF),
        cost_estimate=pl.CostEstimate(
            flops=16 * 64 * C, bytes_accessed=700_000, transcendentals=0
        ),
        compiler_params=pltpu.CompilerParams(vmem_limit_bytes=8 << 20),
        name="sum_heads",
    )(terms)


def copy_kernel(source, target):
    tiles = undense(source[...].astype(F32))
    for row in range(4):
        target[:, row] = tiles[:, row * 4 : row * 4 + 4].astype(BF)


def copied(array):
    return pl.pallas_call(
        copy_kernel,
        out_shape=jax.ShapeDtypeStruct((16, 4, 4, C), BF),
        compiler_params=pltpu.CompilerParams(vmem_limit_bytes=8 << 20),
        cost_estimate=pl.CostEstimate(flops=0, bytes_accessed=400_000, transcendentals=0),
        name="copied",
    )(array)


def nearest_plane(y, h, c, l):
    depth = 8 * h + l + 2 * y - 4 + c
    return l // 2, depth // 8, c, depth % 8


def plan(latent, conv_weight, conv_gain, qkv_weight, qk_gain, out_weight):
    core = lax.axis_index("c")
    first = core == 0
    core = core.astype(jnp.int32).reshape(1)
    tiles = exchange(latent, DEPTH)

    gains = qk_gain.reshape(2, 1, 64)
    gains = jnp.concatenate([jnp.pad(gains, ((0, 0), (0, 0), (0, 64))), jnp.pad(gains, ((0, 0), (0, 0), (64, 0)))], 1)
    gains = jnp.pad(gains.reshape(4, 128), ((0, 12), (0, C - 128)))
    packed = jnp.concatenate([qkv_weight.reshape(192, C), out_weight, gains], 0)
    near = move(packed, ("y", "h", "c", "l"), nearest_plane)
    far = swap(near)
    near, far = jnp.where(first, near, far), jnp.where(first, far, near)

    conv_gain = jnp.pad(conv_gain, ((0, 6), (0, 0)))

    own = tiles.reshape(2, 8, 4, 4, C).transpose(1, 3, 0, 2, 4).reshape(32, 8, C)
    edge = move(
        jnp.where(first, own[:, 0:2], own[:, 6:8]), ("y", "c"), lambda y, c: (y - 1 + 2 * c, 1 - c)
    )
    other = swap(own)
    edge = edge.reshape(64, C)
    left, right = border(core, own, other, edge)
    before = move(right, ("x",), lambda x: (x + 1,))
    after = move(left, ("x",), lambda x: (x - 1,))

    feature_tiles, pooled = conv_stack(core, own, other, edge, before, after, conv_weight, conv_gain)

    tokens = exchange(pooled, ("x", "y")).reshape(1024, C)
    features = exchange(feature_tiles, DEPTH)

    query, pair = heads(tokens, near, far)
    pair_far = swap(pair)
    features = copied(features)
    terms = attend(query, pair, pair_far, tokens, near, far)
    terms = exchange(terms, PLANE)
    mixed = sum_heads(terms)
    mixed = move(
        mixed,
        ("y", "h", "c", "x", "l"),
        lambda y, h, c, x, l: (2 * h + l // 4, (l // 2) % 2, l % 2, x, 2 * y + c),
    )
    return (features, mixed.reshape(1, 32, 2, C))


def solution(mesh):
    planes = Mesh(mesh.devices.reshape(tuple(SIZES.values())), tuple(SIZES))
    placed = (
        P(None, ROW, COL, None),
        P(),
        P(),
        P(None, COL, None),
        P(None, COL),
        P(COL, None),
    )
    return jax.shard_map(
        plan,
        mesh=planes,
        in_specs=placed,
        out_specs=(P(None, ROW, COL, None), P(ROW, None, COL, None)),
        check_vma=False,
    )
```

```python
import math

import jax
import jax.numpy as jnp
from jax import lax
from jax.experimental import pallas as pl
from jax.experimental.pallas import tpu as pltpu
from jax.sharding import Mesh
from jax.sharding import PartitionSpec as P


SIZES = {"y": 4, "h": 2, "c": 2, "x": 4, "l": 8}
ROW = ("y", "h", "c")
COL = ("x", "l")
DEPTH = ("h", "l")
PLANE = ("x", "y", "c")
C = 320
BF = jnp.bfloat16
F32 = jnp.float32


def move(array, axes, target):
    sizes = [SIZES[axis] for axis in axes]
    pairs = []
    count = 1
    for size in sizes:
        count *= size
    for index in range(count):
        rest, place = index, []
        for size in reversed(sizes):
            place.insert(0, rest % size)
            rest //= size
        flat = 0
        for size, value in zip(sizes, target(*place)):
            flat = flat * size + value % size
        pairs.append((index, flat))
    return lax.ppermute(array, axes, pairs)


def exchange(array, axes):
    return lax.all_to_all(array, axes, split_axis=0, concat_axis=0, tiled=True)


def swap(array):
    return lax.ppermute(array, "c", [(0, 1), (1, 0)])


def dot(left, right):
    return jnp.dot(left, right, preferred_element_type=F32)


def dot_t(left, right):
    return lax.dot_general(left, right, (((1,), (1,)), ((), ())), preferred_element_type=F32)


def dense(array):
    half = array.shape[-2] // 2
    tail = array[..., 256:C]
    tail = jnp.concatenate([tail[..., 0:half, :], tail[..., half:, :]], -1)
    return jnp.concatenate([array[..., 0:128], array[..., 128:256], tail], -2)


def undense(array):
    rows = array.shape[-2] * 2 // 5
    tail = array[..., 2 * rows :, :]
    tail = jnp.concatenate([tail[..., 0:64], tail[..., 64:128]], -2)
    return jnp.concatenate([array[..., 0:rows, :], array[..., rows : 2 * rows, :], tail], -1)


def picked(core, first, count, own, other, edge):
    place = lax.broadcasted_iota(jnp.int32, (count * 16, 1), 0)
    column = first + (place >> 4)
    row = ((place >> 3) & 1) * 8 + (place & 7) + core * 4 - 2
    local = column * 8 + ((row >> 3) & 1) * 4 + (row & 3)
    near = jnp.where(((row >> 2) & 1) == core, local, local + 256)
    source = jnp.where((row < 0) | (row > 15), 512 + column * 2 + (row & 1), near)
    at = lax.broadcasted_iota(jnp.int32, (count * 16, 576), 1)
    choice = (at == source).astype(F32).astype(BF)
    rows = dot(choice[:, 0:256], own[...].reshape(256, C))
    rows = rows + dot(choice[:, 256:512], other[...].reshape(256, C))
    return rows + dot(choice[:, 512:576], edge[...])


def border_kernel(core, own, other, edge, left_out, right_out):
    left_out[...] = picked(core[0], 0, 2, own, other, edge).astype(BF)
    right_out[...] = picked(core[0], 30, 2, own, other, edge).astype(BF)


def border(core, own, other, edge):
    return pl.pallas_call(
        border_kernel,
        out_shape=(jax.ShapeDtypeStruct((32, C), BF),) * 2,
        in_specs=[pl.BlockSpec(memory_space=pltpu.SMEM)] + [pl.BlockSpec(memory_space=pltpu.VMEM)] * 3,
        compiler_params=pltpu.CompilerParams(vmem_limit_bytes=8 << 20),
        cost_estimate=pl.CostEstimate(
            flops=2 * 64 * 576 * C, bytes_accessed=400_000, transcendentals=0
        ),
        name="border",
    )(core, own, other, edge)


def packed_rows(array, shift):
    pairs = array.reshape(array.shape[0] // 16, 2, 8, C)
    sub = lax.broadcasted_iota(jnp.int32, pairs[:, 0].shape, 1)
    upper = pltpu.roll(pairs[:, 0], (8 - shift) % 8, 1)
    lower = pltpu.roll(pairs[:, 1], 4 - shift, 1)
    return jnp.where(sub < 4, upper, lower).reshape(array.shape[0] // 2, C)


def conv_kernel(
    core,
    own,
    other,
    edge,
    before,
    after,
    gains,
    stored,
    feat_out,
    pool_out,
    held,
    act,
    taps,
    taps_odd,
    kernels,
    arrived,
    pool,
    sent,
):
    fetches = []
    for layer in range(2):
        for b in range(3):
            fetch = pltpu.make_async_copy(
                stored.at[layer, :, b], kernels.at[layer, b], arrived.at[3 * layer + b]
            )
            fetch.start()
            fetches.append(fetch)

    def activation(wide, layer):
        factor = lax.rsqrt(jnp.mean(wide * wide, axis=-1, keepdims=True) + 1e-06)
        scaled = wide * factor * gains[layer : layer + 1]
        return scaled * jax.nn.sigmoid(scaled)

    def tap(rows, layer, b):
        fetches[3 * layer + b].wait()
        return dot(rows, kernels[layer, b].reshape(3 * C, C))

    held[0:32] = before[...].astype(F32)
    held[32:544] = picked(core[0], 0, 32, own, other, edge)
    held[544:576] = after[...].astype(F32)
    act[0:576] = activation(held[0:576], 0)
    act[576:592] = jnp.zeros((16, C), F32)
    for a in range(3):
        taps[:, a * C : (a + 1) * C] = act[a : a + 576].astype(BF)
    total = tap(taps[0:544], 0, 0) + tap(taps[16:560], 0, 1) + tap(taps[32:576], 0, 2)
    held[576:592] = jnp.zeros((16, C), F32)
    middle = (held[17:561] + total).astype(BF).astype(F32)
    center = packed_rows(middle, 1)[8:264]
    wide = activation(middle, 1)
    for a in range(3):
        rows = packed_rows(wide, a)
        taps[0:272, a * C : (a + 1) * C] = rows.astype(BF)
        taps_odd[:, a * C : (a + 1) * C] = rows[8:264].astype(BF)
    total = tap(taps[0:256], 1, 0) + tap(taps_odd[...], 1, 1) + tap(taps[16:272], 1, 2)
    fresh = (center + total).astype(BF)
    place = lax.broadcasted_iota(jnp.int32, (64, 256), 1)
    index = lax.broadcasted_iota(jnp.int32, (64, 256), 0)
    same = ((place >> 4) == (index >> 3) * 2 + (index & 1)) & (
        ((place >> 1) & 3) == ((index >> 2) & 1) * 2 + ((index >> 1) & 1)
    )
    pooled = dot(jnp.where(same, 0.25, 0.0).astype(BF), fresh).astype(BF)
    pool[...] = pooled
    copies = [pltpu.make_async_copy(pool, pool_out.at[slot], sent.at[slot]) for slot in range(16)]
    for copy in copies:
        copy.start()
    feat_out[...] = fresh
    for copy in copies:
        copy.wait()


def conv_stack(core, own, other, edge, before, after, kernels, gains):
    return pl.pallas_call(
        conv_kernel,
        out_shape=(
            jax.ShapeDtypeStruct((256, C), BF),
            jax.ShapeDtypeStruct((16, 64, C), BF),
        ),
        out_specs=(pl.BlockSpec(memory_space=pltpu.VMEM), pl.BlockSpec(memory_space=pltpu.HBM)),
        in_specs=[pl.BlockSpec(memory_space=pltpu.SMEM)]
        + [pl.BlockSpec(memory_space=pltpu.VMEM)] * 6
        + [pl.BlockSpec(memory_space=pltpu.HBM)],
        scratch_shapes=[
            pltpu.VMEM((608, C), F32),
            pltpu.VMEM((608, C), F32),
            pltpu.VMEM((576, 3 * C), BF),
            pltpu.VMEM((256, 3 * C), BF),
            pltpu.VMEM((2, 3, 3, C, C), BF),
            pltpu.SemaphoreType.DMA((6,)),
            pltpu.VMEM((64, C), BF),
            pltpu.SemaphoreType.DMA((16,)),
        ],
        cost_estimate=pl.CostEstimate(
            flops=2 * 1056 * 9 * C * C, bytes_accessed=5_000_000, transcendentals=360_000
        ),
        compiler_params=pltpu.CompilerParams(vmem_limit_bytes=52 << 20),
        name="conv_stack",
    )(core, own, other, edge, before, after, gains, kernels)


def tiled_kernel(fresh, feat_out):
    place = lax.broadcasted_iota(jnp.int32, (256, 256), 1)
    index = lax.broadcasted_iota(jnp.int32, (256, 256), 0)
    source = (((index >> 4) & 7) * 4 + (index & 3)) * 8 + (index >> 7) * 4 + ((index >> 2) & 3)
    tiles = dot((place == source).astype(F32).astype(BF), fresh[...]).reshape(16, 16, C)
    feat_out[...] = dense(tiles).astype(BF)


def tiled(fresh):
    return pl.pallas_call(
        tiled_kernel,
        out_shape=jax.ShapeDtypeStruct((16, 40, 128), BF),
        compiler_params=pltpu.CompilerParams(vmem_limit_bytes=8 << 20),
        cost_estimate=pl.CostEstimate(
            flops=2 * 256 * 256 * C, bytes_accessed=400_000, transcendentals=0
        ),
        name="tiled",
    )(fresh)


def norm(projected, gain):
    factor = lax.rsqrt(jnp.mean(projected * projected, axis=-1, keepdims=True) + 1e-06)
    return (projected * factor * gain).astype(BF)


def heads_kernel(tokens, near, far, query_out, pair_out):
    def both(start):
        return jnp.concatenate([near[start : start + 64], far[start : start + 64]], 0)

    matrix = jnp.concatenate([both(0), both(64), both(128)], 0)
    projected = dot_t(tokens[...], matrix)
    query_gain = near[256:257, 0:128].astype(F32) + far[257:258, 0:128].astype(F32)
    key_gain = near[258:259, 0:128].astype(F32) + far[259:260, 0:128].astype(F32)
    query_out[...] = norm(projected[:, 0:128], query_gain * (128 ** (-0.5) * math.log2(math.e)))
    pair_out[:, 0:128] = norm(projected[:, 128:256], key_gain)
    pair_out[:, 128:256] = projected[:, 256:384].astype(BF)


def heads(tokens, near, far):
    return pl.pallas_call(
        heads_kernel,
        out_shape=(
            jax.ShapeDtypeStruct((1024, 128), BF),
            jax.ShapeDtypeStruct((1024, 256), BF),
        ),
        cost_estimate=pl.CostEstimate(
            flops=2 * 1024 * 384 * C, bytes_accessed=2_000_000, transcendentals=2048
        ),
        compiler_params=pltpu.CompilerParams(vmem_limit_bytes=16 << 20),
        name="heads",
    )(tokens, near, far)


def attend_kernel(query, pair, pair_far, tokens, near, far, terms_out, ready, sent):
    head_out = jnp.concatenate([near[192:256], far[192:256]], 0)

    def send(step):
        part = pl.ds(pl.multiple_of(step * 8, 8), 8)
        return pltpu.make_async_copy(ready.at[part], terms_out.at[part], sent.at[step])

    def one_block(step, _):
        rows = pl.ds(pl.multiple_of(step * 256, 256), 256)
        asked = query[rows]
        scores = dot_t(asked, pair[:, 0:128])
        scores_far = dot_t(asked, pair_far[:, 0:128])
        top = jnp.maximum(
            jnp.max(scores, axis=1, keepdims=True), jnp.max(scores_far, axis=1, keepdims=True)
        )
        shifted = jnp.exp2(scores - top)
        shifted_far = jnp.exp2(scores_far - top)
        total = jnp.sum(shifted, axis=1, keepdims=True) + jnp.sum(shifted_far, axis=1, keepdims=True)
        attended = dot(shifted.astype(BF), pair[:, 128:256])
        attended = attended + dot(shifted_far.astype(BF), pair_far[:, 128:256])
        attended = (attended / total).astype(BF)
        terms = dot(attended, head_out) + tokens[rows].astype(F32) * 0.0625
        for column in range(8):
            parts = [
                terms[y * 64 + column * 8 : y * 64 + column * 8 + 8] for y in range(4)
            ]
            ready[step * 8 + column] = dense(jnp.concatenate(parts, 0)).astype(BF)
        send(step).start()
        return 0

    lax.fori_loop(0, 4, one_block, 0, unroll=True)
    for step in range(4):
        send(step).wait()


def attend(query, pair, pair_far, tokens, near, far):
    return pl.pallas_call(
        attend_kernel,
        out_shape=jax.ShapeDtypeStruct((32, 80, 128), BF),
        out_specs=pl.BlockSpec(memory_space=pltpu.HBM),
        scratch_shapes=[pltpu.VMEM((32, 80, 128), BF), pltpu.SemaphoreType.DMA((4,))],
        cost_estimate=pl.CostEstimate(
            flops=2 * 1024 * 128 * (2 * 2048 + C),
            bytes_accessed=3_000_000,
            transcendentals=1024 * 2048,
        ),
        compiler_params=pltpu.CompilerParams(vmem_limit_bytes=24 << 20),
        name="attend",
    )(query, pair, pair_far, tokens, near, far)


def sum_kernel(terms, mixed_out):
    total = terms[0:2].astype(F32)
    for head in range(1, 16):
        total = total + terms[2 * head : 2 * head + 2].astype(F32)
    total = undense(total).reshape(64, C)
    for half in range(2):
        for strip in range(8):
            part = total[half * 32 + strip * 4 : half * 32 + strip * 4 + 4].reshape(2, 2, C)
            at = strip * 4 + half * 2
            mixed_out[at : at + 2] = part.astype(BF)


def sum_heads(terms):
    return pl.pallas_call(
        sum_kernel,
        out_shape=jax.ShapeDtypeStruct((32, 2, C), BF),
        cost_estimate=pl.CostEstimate(
            flops=16 * 64 * C, bytes_accessed=700_000, transcendentals=0
        ),
        compiler_params=pltpu.CompilerParams(vmem_limit_bytes=8 << 20),
        name="sum_heads",
    )(terms)


def copy_kernel(source, target):
    tiles = undense(source[...].astype(F32))
    for row in range(4):
        target[:, row] = tiles[:, row * 4 : row * 4 + 4].astype(BF)


def copied(array):
    return pl.pallas_call(
        copy_kernel,
        out_shape=jax.ShapeDtypeStruct((16, 4, 4, C), BF),
        compiler_params=pltpu.CompilerParams(vmem_limit_bytes=8 << 20),
        cost_estimate=pl.CostEstimate(flops=0, bytes_accessed=400_000, transcendentals=0),
        name="copied",
    )(array)


def nearest_plane(y, h, c, l):
    depth = 8 * h + l + 2 * y - 4 + c
    return l // 2, depth // 8, c, depth % 8


def plan(latent, conv_weight, conv_gain, qkv_weight, qk_gain, out_weight):
    core = lax.axis_index("c")
    first = core == 0
    core = core.astype(jnp.int32).reshape(1)
    tiles = exchange(latent, DEPTH)

    gains = qk_gain.reshape(2, 1, 64)
    gains = jnp.concatenate([jnp.pad(gains, ((0, 0), (0, 0), (0, 64))), jnp.pad(gains, ((0, 0), (0, 0), (64, 0)))], 1)
    gains = jnp.pad(gains.reshape(4, 128), ((0, 12), (0, C - 128)))
    packed = jnp.concatenate([qkv_weight.reshape(192, C), out_weight, gains], 0)
    near = move(packed, ("y", "h", "c", "l"), nearest_plane)
    far = swap(near)
    near, far = jnp.where(first, near, far), jnp.where(first, far, near)

    conv_gain = jnp.pad(conv_gain, ((0, 6), (0, 0)))

    own = tiles.reshape(2, 8, 4, 4, C).transpose(1, 3, 0, 2, 4).reshape(32, 8, C)
    edge = move(
        jnp.where(first, own[:, 0:2], own[:, 6:8]), ("y", "c"), lambda y, c: (y - 1 + 2 * c, 1 - c)
    )
    other = swap(own)
    edge = edge.reshape(64, C)
    left, right = border(core, own, other, edge)
    before = move(right, ("x",), lambda x: (x + 1,))
    after = move(left, ("x",), lambda x: (x - 1,))

    fresh, pooled = conv_stack(core, own, other, edge, before, after, conv_weight, conv_gain)

    tokens = exchange(pooled, ("x", "y")).reshape(1024, C)
    feature_tiles = tiled(fresh)
    features = exchange(feature_tiles, DEPTH)

    query, pair = heads(tokens, near, far)
    pair_far = swap(pair)
    features = copied(features)
    terms = attend(query, pair, pair_far, tokens, near, far)
    terms = exchange(terms, PLANE)
    mixed = sum_heads(terms)
    mixed = move(
        mixed,
        ("y", "h", "c", "x", "l"),
        lambda y, h, c, x, l: (2 * h + l // 4, (l // 2) % 2, l % 2, x, 2 * y + c),
    )
    return (features, mixed.reshape(1, 32, 2, C))


def solution(mesh):
    planes = Mesh(mesh.devices.reshape(tuple(SIZES.values())), tuple(SIZES))
    placed = (
        P(None, ROW, COL, None),
        P(),
        P(),
        P(None, COL, None),
        P(None, COL),
        P(COL, None),
    )
    return jax.shard_map(
        plan,
        mesh=planes,
        in_specs=placed,
        out_specs=(P(None, ROW, COL, None), P(ROW, None, COL, None)),
        check_vma=False,
    )
```

```python
import math

import jax
import jax.numpy as jnp
from jax import lax
from jax.experimental import pallas as pl
from jax.experimental.pallas import tpu as pltpu
from jax.sharding import Mesh
from jax.sharding import PartitionSpec as P


SIZES = {"y": 4, "h": 2, "c": 2, "x": 4, "l": 8}
ROW = ("y", "h", "c")
COL = ("x", "l")
DEPTH = ("h", "l")
PLANE = ("x", "y", "c")
C = 320
BF = jnp.bfloat16
F32 = jnp.float32


def move(array, axes, target):
    sizes = [SIZES[axis] for axis in axes]
    pairs = []
    count = 1
    for size in sizes:
        count *= size
    for index in range(count):
        rest, place = index, []
        for size in reversed(sizes):
            place.insert(0, rest % size)
            rest //= size
        flat = 0
        for size, value in zip(sizes, target(*place)):
            flat = flat * size + value % size
        pairs.append((index, flat))
    return lax.ppermute(array, axes, pairs)


def exchange(array, axes):
    return lax.all_to_all(array, axes, split_axis=0, concat_axis=0, tiled=True)


def swap(array):
    return lax.ppermute(array, "c", [(0, 1), (1, 0)])


def dot(left, right):
    return jnp.dot(left, right, preferred_element_type=F32)


def dot_t(left, right):
    return lax.dot_general(left, right, (((1,), (1,)), ((), ())), preferred_element_type=F32)


def dense(array):
    half = array.shape[-2] // 2
    tail = array[..., 256:C]
    tail = jnp.concatenate([tail[..., 0:half, :], tail[..., half:, :]], -1)
    return jnp.concatenate([array[..., 0:128], array[..., 128:256], tail], -2)


def undense(array):
    rows = array.shape[-2] * 2 // 5
    tail = array[..., 2 * rows :, :]
    tail = jnp.concatenate([tail[..., 0:64], tail[..., 64:128]], -2)
    return jnp.concatenate([array[..., 0:rows, :], array[..., rows : 2 * rows, :], tail], -1)


def picked(core, first, count, own, other, edge):
    place = lax.broadcasted_iota(jnp.int32, (count * 16, 1), 0)
    column = first + (place >> 4)
    row = ((place >> 3) & 1) * 8 + (place & 7) + core * 4 - 2
    local = column * 8 + ((row >> 3) & 1) * 4 + (row & 3)
    near = jnp.where(((row >> 2) & 1) == core, local, local + 256)
    source = jnp.where((row < 0) | (row > 15), 512 + column * 2 + (row & 1), near)
    at = lax.broadcasted_iota(jnp.int32, (count * 16, 576), 1)
    choice = (at == source).astype(F32).astype(BF)
    rows = dot(choice[:, 0:256], own[...].reshape(256, C))
    rows = rows + dot(choice[:, 256:512], other[...].reshape(256, C))
    return rows + dot(choice[:, 512:576], edge[...])


def border_kernel(core, own, other, edge, left_out, right_out):
    left_out[...] = picked(core[0], 0, 2, own, other, edge).astype(BF)
    right_out[...] = picked(core[0], 30, 2, own, other, edge).astype(BF)


def border(core, own, other, edge):
    return pl.pallas_call(
        border_kernel,
        out_shape=(jax.ShapeDtypeStruct((32, C), BF),) * 2,
        in_specs=[pl.BlockSpec(memory_space=pltpu.SMEM)] + [pl.BlockSpec(memory_space=pltpu.VMEM)] * 3,
        compiler_params=pltpu.CompilerParams(vmem_limit_bytes=8 << 20),
        cost_estimate=pl.CostEstimate(
            flops=2 * 64 * 576 * C, bytes_accessed=400_000, transcendentals=0
        ),
        name="border",
    )(core, own, other, edge)


def packed_rows(array, shift):
    pairs = array.reshape(array.shape[0] // 16, 2, 8, C)
    sub = lax.broadcasted_iota(jnp.int32, pairs[:, 0].shape, 1)
    upper = pltpu.roll(pairs[:, 0], (8 - shift) % 8, 1)
    lower = pltpu.roll(pairs[:, 1], 4 - shift, 1)
    return jnp.where(sub < 4, upper, lower).reshape(array.shape[0] // 2, C)


def conv_kernel(
    core,
    own,
    other,
    edge,
    before,
    after,
    gains,
    stored,
    feat_out,
    pool_out,
    held,
    act,
    taps,
    taps_odd,
    kernels,
    arrived,
    pool,
    sent,
):
    fetches = []
    for layer in range(2):
        for b in range(3):
            fetch = pltpu.make_async_copy(
                stored.at[layer, :, b], kernels.at[layer, b], arrived.at[3 * layer + b]
            )
            fetch.start()
            fetches.append(fetch)

    def activation(wide, layer):
        factor = lax.rsqrt(jnp.mean(wide * wide, axis=-1, keepdims=True) + 1e-06)
        scaled = wide * factor * gains[layer : layer + 1]
        return scaled * jax.nn.sigmoid(scaled)

    def tap(rows, layer, b):
        fetches[3 * layer + b].wait()
        return dot(rows, kernels[layer, b].reshape(3 * C, C))

    held[0:32] = before[...].astype(F32)
    held[32:544] = picked(core[0], 0, 32, own, other, edge)
    held[544:576] = after[...].astype(F32)
    act[0:576] = activation(held[0:576], 0)
    act[576:592] = jnp.zeros((16, C), F32)
    for a in range(3):
        taps[:, a * C : (a + 1) * C] = act[a : a + 576].astype(BF)
    total = tap(taps[0:544], 0, 0) + tap(taps[16:560], 0, 1) + tap(taps[32:576], 0, 2)
    held[576:592] = jnp.zeros((16, C), F32)
    middle = (held[17:561] + total).astype(BF).astype(F32)
    center = packed_rows(middle, 1)[8:264]
    wide = activation(middle, 1)
    for a in range(3):
        rows = packed_rows(wide, a)
        taps[0:272, a * C : (a + 1) * C] = rows.astype(BF)
        taps_odd[:, a * C : (a + 1) * C] = rows[8:264].astype(BF)
    total = tap(taps[0:256], 1, 0) + tap(taps_odd[...], 1, 1) + tap(taps[16:272], 1, 2)
    fresh = (center + total).astype(BF)
    place = lax.broadcasted_iota(jnp.int32, (64, 256), 1)
    index = lax.broadcasted_iota(jnp.int32, (64, 256), 0)
    same = ((place >> 4) == (index >> 3) * 2 + (index & 1)) & (
        ((place >> 1) & 3) == ((index >> 2) & 1) * 2 + ((index >> 1) & 1)
    )
    pooled = dot(jnp.where(same, 0.25, 0.0).astype(BF), fresh)
    pool[...] = dense(pooled).astype(BF)
    copies = [pltpu.make_async_copy(pool, pool_out.at[slot], sent.at[slot]) for slot in range(16)]
    for copy in copies:
        copy.start()
    feat_out[...] = fresh
    for copy in copies:
        copy.wait()


def conv_stack(core, own, other, edge, before, after, kernels, gains):
    return pl.pallas_call(
        conv_kernel,
        out_shape=(
            jax.ShapeDtypeStruct((256, C), BF),
            jax.ShapeDtypeStruct((16, 160, 128), BF),
        ),
        out_specs=(pl.BlockSpec(memory_space=pltpu.VMEM), pl.BlockSpec(memory_space=pltpu.HBM)),
        in_specs=[pl.BlockSpec(memory_space=pltpu.SMEM)]
        + [pl.BlockSpec(memory_space=pltpu.VMEM)] * 6
        + [pl.BlockSpec(memory_space=pltpu.HBM)],
        scratch_shapes=[
            pltpu.VMEM((608, C), F32),
            pltpu.VMEM((608, C), F32),
            pltpu.VMEM((576, 3 * C), BF),
            pltpu.VMEM((256, 3 * C), BF),
            pltpu.VMEM((2, 3, 3, C, C), BF),
            pltpu.SemaphoreType.DMA((6,)),
            pltpu.VMEM((160, 128), BF),
            pltpu.SemaphoreType.DMA((16,)),
        ],
        cost_estimate=pl.CostEstimate(
            flops=2 * 1056 * 9 * C * C, bytes_accessed=5_000_000, transcendentals=360_000
        ),
        compiler_params=pltpu.CompilerParams(vmem_limit_bytes=52 << 20),
        name="conv_stack",
    )(core, own, other, edge, before, after, gains, kernels)


def tiled_kernel(fresh, feat_out):
    place = lax.broadcasted_iota(jnp.int32, (256, 256), 1)
    index = lax.broadcasted_iota(jnp.int32, (256, 256), 0)
    source = (((index >> 4) & 7) * 4 + (index & 3)) * 8 + (index >> 7) * 4 + ((index >> 2) & 3)
    tiles = dot((place == source).astype(F32).astype(BF), fresh[...]).reshape(16, 16, C)
    feat_out[...] = dense(tiles).astype(BF)


def tiled(fresh):
    return pl.pallas_call(
        tiled_kernel,
        out_shape=jax.ShapeDtypeStruct((16, 40, 128), BF),
        compiler_params=pltpu.CompilerParams(vmem_limit_bytes=8 << 20),
        cost_estimate=pl.CostEstimate(
            flops=2 * 256 * 256 * C, bytes_accessed=400_000, transcendentals=0
        ),
        name="tiled",
    )(fresh)


def norm(projected, gain):
    factor = lax.rsqrt(jnp.mean(projected * projected, axis=-1, keepdims=True) + 1e-06)
    return (projected * factor * gain).astype(BF)


def heads_kernel(tokens, near, far, query_out, pair_out):
    def both(start):
        return jnp.concatenate([near[start : start + 64], far[start : start + 64]], 0)

    matrix = jnp.concatenate([both(0), both(64), both(128)], 0)
    wide = jnp.concatenate(
        [tokens[:, 0:64].reshape(1024, 128), tokens[:, 64:128].reshape(1024, 128)], 1
    )
    tail = tokens[:, 128:160].reshape(512, 128)
    none = jnp.zeros((384, 64), BF)
    upper = dot_t(tail, jnp.concatenate([matrix[:, 256:C], none], 1)).reshape(16, 32, 384)
    lower = dot_t(tail, jnp.concatenate([none, matrix[:, 256:C]], 1)).reshape(16, 32, 384)
    projected = dot_t(wide, matrix[:, 0:256])
    projected = projected + jnp.concatenate([upper, lower], 1).reshape(1024, 384)
    query_gain = near[256:257, 0:128].astype(F32) + far[257:258, 0:128].astype(F32)
    key_gain = near[258:259, 0:128].astype(F32) + far[259:260, 0:128].astype(F32)
    query_out[...] = norm(projected[:, 0:128], query_gain * (128 ** (-0.5) * math.log2(math.e)))
    pair_out[:, 0:128] = norm(projected[:, 128:256], key_gain)
    pair_out[:, 128:256] = projected[:, 256:384].astype(BF)


def heads(tokens, near, far):
    return pl.pallas_call(
        heads_kernel,
        out_shape=(
            jax.ShapeDtypeStruct((1024, 128), BF),
            jax.ShapeDtypeStruct((1024, 256), BF),
        ),
        cost_estimate=pl.CostEstimate(
            flops=2 * 1024 * 384 * C, bytes_accessed=2_000_000, transcendentals=2048
        ),
        compiler_params=pltpu.CompilerParams(vmem_limit_bytes=16 << 20),
        name="heads",
    )(tokens, near, far)


def attend_kernel(query, pair, pair_far, tokens, near, far, terms_out, ready, sent):
    head_out = jnp.concatenate([near[192:256], far[192:256]], 0)

    def send(step):
        part = pl.ds(pl.multiple_of(step * 8, 8), 8)
        return pltpu.make_async_copy(ready.at[part], terms_out.at[part], sent.at[step])

    def one_block(step, _):
        rows = pl.ds(pl.multiple_of(step * 256, 256), 256)
        asked = query[rows]
        scores = dot_t(asked, pair[:, 0:128])
        scores_far = dot_t(asked, pair_far[:, 0:128])
        top = jnp.maximum(
            jnp.max(scores, axis=1, keepdims=True), jnp.max(scores_far, axis=1, keepdims=True)
        )
        shifted = jnp.exp2(scores - top)
        shifted_far = jnp.exp2(scores_far - top)
        total = jnp.sum(shifted, axis=1, keepdims=True) + jnp.sum(shifted_far, axis=1, keepdims=True)
        attended = dot(shifted.astype(BF), pair[:, 128:256])
        attended = attended + dot(shifted_far.astype(BF), pair_far[:, 128:256])
        attended = (attended / total).astype(BF)
        terms = dot(attended, head_out) + undense(
            tokens[pl.ds(step * 4, 4)].astype(F32)
        ).reshape(256, C) * 0.0625
        for column in range(8):
            parts = [
                terms[y * 64 + column * 8 : y * 64 + column * 8 + 8] for y in range(4)
            ]
            ready[step * 8 + column] = dense(jnp.concatenate(parts, 0)).astype(BF)
        send(step).start()
        return 0

    lax.fori_loop(0, 4, one_block, 0, unroll=True)
    for step in range(4):
        send(step).wait()


def attend(query, pair, pair_far, tokens, near, far):
    return pl.pallas_call(
        attend_kernel,
        out_shape=jax.ShapeDtypeStruct((32, 80, 128), BF),
        out_specs=pl.BlockSpec(memory_space=pltpu.HBM),
        scratch_shapes=[pltpu.VMEM((32, 80, 128), BF), pltpu.SemaphoreType.DMA((4,))],
        cost_estimate=pl.CostEstimate(
            flops=2 * 1024 * 128 * (2 * 2048 + C),
            bytes_accessed=3_000_000,
            transcendentals=1024 * 2048,
        ),
        compiler_params=pltpu.CompilerParams(vmem_limit_bytes=24 << 20),
        name="attend",
    )(query, pair, pair_far, tokens, near, far)


def sum_kernel(terms, mixed_out):
    total = terms[0:2].astype(F32)
    for head in range(1, 16):
        total = total + terms[2 * head : 2 * head + 2].astype(F32)
    total = undense(total).reshape(64, C)
    for half in range(2):
        for strip in range(8):
            part = total[half * 32 + strip * 4 : half * 32 + strip * 4 + 4].reshape(2, 2, C)
            at = strip * 4 + half * 2
            mixed_out[at : at + 2] = part.astype(BF)


def sum_heads(terms):
    return pl.pallas_call(
        sum_kernel,
        out_shape=jax.ShapeDtypeStruct((32, 2, C), BF),
        cost_estimate=pl.CostEstimate(
            flops=16 * 64 * C, bytes_accessed=700_000, transcendentals=0
        ),
        compiler_params=pltpu.CompilerParams(vmem_limit_bytes=8 << 20),
        name="sum_heads",
    )(terms)


def copy_kernel(source, target):
    tiles = undense(source[...].astype(F32))
    for row in range(4):
        target[:, row] = tiles[:, row * 4 : row * 4 + 4].astype(BF)


def copied(array):
    return pl.pallas_call(
        copy_kernel,
        out_shape=jax.ShapeDtypeStruct((16, 4, 4, C), BF),
        compiler_params=pltpu.CompilerParams(vmem_limit_bytes=8 << 20),
        cost_estimate=pl.CostEstimate(flops=0, bytes_accessed=400_000, transcendentals=0),
        name="copied",
    )(array)


def nearest_plane(y, h, c, l):
    depth = 8 * h + l + 2 * y - 4 + c
    return l // 2, depth // 8, c, depth % 8


def plan(latent, conv_weight, conv_gain, qkv_weight, qk_gain, out_weight):
    core = lax.axis_index("c")
    first = core == 0
    core = core.astype(jnp.int32).reshape(1)
    tiles = exchange(latent, DEPTH)

    gains = qk_gain.reshape(2, 1, 64)
    gains = jnp.concatenate([jnp.pad(gains, ((0, 0), (0, 0), (0, 64))), jnp.pad(gains, ((0, 0), (0, 0), (64, 0)))], 1)
    gains = jnp.pad(gains.reshape(4, 128), ((0, 12), (0, C - 128)))
    packed = jnp.concatenate([qkv_weight.reshape(192, C), out_weight, gains], 0)
    near = move(packed, ("y", "h", "c", "l"), nearest_plane)
    far = swap(near)
    near, far = jnp.where(first, near, far), jnp.where(first, far, near)

    conv_gain = jnp.pad(conv_gain, ((0, 6), (0, 0)))

    own = tiles.reshape(2, 8, 4, 4, C).transpose(1, 3, 0, 2, 4).reshape(32, 8, C)
    edge = move(
        jnp.where(first, own[:, 0:2], own[:, 6:8]), ("y", "c"), lambda y, c: (y - 1 + 2 * c, 1 - c)
    )
    other = swap(own)
    edge = edge.reshape(64, C)
    left, right = border(core, own, other, edge)
    before = move(right, ("x",), lambda x: (x + 1,))
    after = move(left, ("x",), lambda x: (x - 1,))

    fresh, pooled = conv_stack(core, own, other, edge, before, after, conv_weight, conv_gain)

    tokens = exchange(pooled, ("x", "y"))
    feature_tiles = tiled(fresh)
    features = exchange(feature_tiles, DEPTH)

    query, pair = heads(tokens, near, far)
    pair_far = swap(pair)
    features = copied(features)
    terms = attend(query, pair, pair_far, tokens, near, far)
    terms = exchange(terms, PLANE)
    mixed = sum_heads(terms)
    mixed = move(
        mixed,
        ("y", "h", "c", "x", "l"),
        lambda y, h, c, x, l: (2 * h + l // 4, (l // 2) % 2, l % 2, x, 2 * y + c),
    )
    return (features, mixed.reshape(1, 32, 2, C))


def solution(mesh):
    planes = Mesh(mesh.devices.reshape(tuple(SIZES.values())), tuple(SIZES))
    placed = (
        P(None, ROW, COL, None),
        P(),
        P(),
        P(None, COL, None),
        P(None, COL),
        P(COL, None),
    )
    return jax.shard_map(
        plan,
        mesh=planes,
        in_specs=placed,
        out_specs=(P(None, ROW, COL, None), P(ROW, None, COL, None)),
        check_vma=False,
    )
```
